512 devices in a mesh: nodes: 64 (over x, z), heads: 8 (over y, core).
Axes of the slice: x: 4, y: 4, z: 16, core: 2. Of those that a mesh axis runs over, the one named last changes fastest.
Arguments:
- hidden: bfloat16 [64, 7168], P('nodes'), may hold values from -6 to 6
- norm_gain: float32 [7168], replicated, may hold values from 0.1 to 1.9
- qkv_weight: bfloat16 [7168, 56, 384], P('nodes', 'heads'), may hold values from -0.0625 to 0.0625
- out_weight: bfloat16 [7168, 7168], P('heads', 'nodes'), may hold values from -0.0625 to 0.0625
- prefix_keys: bfloat16 [256, 128, 56, 128], P('nodes', None, 'heads'), may hold values from -1000 to 1000
- prefix_values: bfloat16 [256, 128, 56, 128], P('nodes', None, 'heads'), may hold values from -3 to 3
- leaf_keys: bfloat16 [64, 64, 56, 128], P('nodes', None, 'heads'), may hold values from -1000 to 1000
- leaf_values: bfloat16 [64, 64, 56, 128], P('nodes', None, 'heads'), may hold values from -3 to 3
- piece_node: int32 [256], replicated, may hold values from 0 to 35, as said below
- mid_parent: int32 [32], replicated, may hold values from 0 to 3
- leaf_parent: int32 [64], replicated, may hold values from 0 to 31
- leaf_len: int32 [64], replicated, may hold values from 1 to 64
- sink_len: int32 [64], replicated, may hold values from 0 to 4
- window_len: int32 [64], replicated, may hold values from 2048 to 4096
Outputs:
- layer_out: bfloat16 [64, 7168], P('heads', 'nodes')
The draws below stay inside these ranges and needn't reach their ends.
Inputs may be any that keep to these rules, and one draw needn't show every extreme that they name: `piece_node`: every root owns some pieces; a middle node may own none.
All inputs are finite; a program needn't handle non-finite values.
Results may differ from the reference program's by a relative error of at most 0.007.
The reference program's roundings to bfloat16 on the way (of `normed` and `attended`) count: a program that leaves them out, or rounds other values in their place, can miss the bound.
Values may be sent and summed in bfloat16 or wider, within the bound.
A program may use at most 64 MiB of HBM per device.

```python
import math
import jax
import jax.numpy as jnp
import numpy as np
from jax import lax

D = 7168
HEADS = 56
HEAD_DIM = 128
SEG_DEV = 4
SEG = 128
LEAF_MAX = 64
ROOTS = 4
MIDS = 32
WINDOW = 4096
SINK_MAX = 4
REQUESTS = 64
PIECES = 256


def draw_keys(key, shape):
    base = jax.random.truncated_normal(key, -6.0, 6.0, shape, jnp.float32) * 0.5
    return base.astype(jnp.bfloat16)


def draw_prefix_keys(key, part):
    inner = jax.random.fold_in(key, 101)
    return draw_keys(inner, (PIECES, SEG, HEADS, HEAD_DIM))


def draw_leaf_keys(key, part):
    inner = jax.random.fold_in(key, 103)
    return draw_keys(inner, (REQUESTS, LEAF_MAX, HEADS, HEAD_DIM))


def draw_piece_node(key, part):
    slots = jnp.arange(PIECES, dtype=jnp.int32)
    split = PIECES * 2 // 3
    middles = ROOTS + MIDS - 1 - (slots - split) % MIDS
    owners = jnp.where(slots < split, slots % ROOTS, middles).astype(jnp.int32)
    shuffled = jax.random.permutation(jax.random.fold_in(key, 5), PIECES)
    return owners[shuffled].astype(jnp.int32)


def with_largest(key, values, largest):
    chosen = jax.random.randint(jax.random.fold_in(key, 3), (), 0, REQUESTS)
    return jnp.where(jnp.arange(REQUESTS, dtype=jnp.int32) == chosen, largest, values).astype(jnp.int32)


def draw_leaf_len(key, part):
    first = jax.random.randint(jax.random.fold_in(key, 1), (REQUESTS,), 1, LEAF_MAX + 1)
    second = jax.random.randint(jax.random.fold_in(key, 2), (REQUESTS,), 1, LEAF_MAX + 1)
    lengths = jnp.maximum(first * second // LEAF_MAX, 1)
    return with_largest(key, lengths, LEAF_MAX)


def draw_sink_len(key, part):
    sinks = jax.random.randint(jax.random.fold_in(key, 21), (REQUESTS,), 0, SINK_MAX + 1)
    return with_largest(jax.random.fold_in(key, 22), sinks, SINK_MAX)


def draw_window_len(key, part):
    windows = jax.random.randint(jax.random.fold_in(key, 31), (REQUESTS,), WINDOW // 2, WINDOW + 1)
    return with_largest(jax.random.fold_in(key, 32), windows, WINDOW)


def plant(values, stream_key, low, high):
    index_at = [jax.random.randint(jax.random.fold_in(stream_key, axis), (), 0, length) for axis, length in enumerate(values.shape)]
    main_axis = values.shape.index(max(values.shape))
    neighbour = index_at[:main_axis] + [(index_at[main_axis] + 1) % values.shape[main_axis]] + index_at[main_axis + 1:]
    return values.at[tuple(index_at)].set(low).at[tuple(neighbour)].set(high)


def level_of(key, extent, cuts, low, high):
    factor_of, own = 1.0, jax.random.fold_in(key, 6)
    for dim, shards_of in cuts:
        steps = jnp.exp(jax.random.uniform(jax.random.fold_in(own, dim), (shards_of,), jnp.float32, low / len(cuts), high / len(cuts)))
        factor_of = factor_of * jnp.repeat(steps, extent[dim] // shards_of).reshape([-1 if axis == dim else 1 for axis in range(len(extent))])
    return factor_of


def rank_bounds(amount, lean):
    portions = [(1 << 20) // math.isqrt(grade ** lean) + 1 for grade in range(1, amount + 1)]
    deviation = 1 + sum(portions) // (1 << 30)
    return np.cumsum(np.array([max(1, weight // deviation) for weight in portions]))


def ranked_ids(key, dims, number_of, skew):
    listing = rank_bounds(number_of, skew)
    ticket = jax.random.randint(jax.random.fold_in(key, 1), dims, 0, int(listing[number_of - 1]))
    grade = jnp.searchsorted(jnp.asarray(listing, jnp.int32), ticket, side="right")
    return jax.random.permutation(jax.random.fold_in(key, 2), number_of)[grade].astype(jnp.int32)


def gaussian(stream_key, shape, width, most, cuts=(), kind=jnp.bfloat16):
    array = jax.random.normal(stream_key, shape, jnp.float32) * width
    if len(cuts) > 0:
        array = level_of(stream_key, shape, cuts, -0.22, 0.18) * array
    return jnp.clip(array, min=-most, max=most).astype(kind)


def setup_inputs(seed: int = 0) -> dict:
    splits = jax.random.split(jax.random.key(seed), 15)
    return {
        "hidden": gaussian(splits[0], (REQUESTS, D), 1.0, 6.0, ((0, 64),)),
        "norm_gain": jnp.clip(1.0 + 0.18 * jax.random.normal(splits[1], (D,), jnp.float32), 0.1, 1.9),
        "qkv_weight": gaussian(splits[2], (D, HEADS, 3 * HEAD_DIM), D ** -0.5, 0.0625, ((0, 64), (1, 8))),
        "out_weight": gaussian(splits[3], (HEADS * HEAD_DIM, D), (HEADS * HEAD_DIM) ** -0.5, 0.0625, ((0, 8), (1, 64))),
        "prefix_keys": draw_prefix_keys(jax.random.fold_in(splits[14], 71), 0),
        "prefix_values": gaussian(splits[5], (PIECES, SEG, HEADS, HEAD_DIM), 0.2, 3.0, ((0, 64), (2, 8))),
        "leaf_keys": draw_leaf_keys(jax.random.fold_in(splits[14], 71), 0),
        "leaf_values": gaussian(splits[7], (REQUESTS, LEAF_MAX, HEADS, HEAD_DIM), 0.2, 3.0, ((0, 64), (2, 8))),
        "piece_node": draw_piece_node(jax.random.fold_in(splits[14], 71), 0),
        "mid_parent": plant(jax.random.randint(splits[9], (MIDS,), 0, ROOTS), jax.random.fold_in(splits[9], 1), 0, ROOTS - 1).astype(jnp.int32),
        "leaf_parent": plant(ranked_ids(splits[10], (REQUESTS,), MIDS, 2), jax.random.fold_in(splits[10], 3), 0, MIDS - 1).astype(jnp.int32),
        "leaf_len": draw_leaf_len(jax.random.fold_in(splits[14], 71), 0),
        "sink_len": draw_sink_len(jax.random.fold_in(splits[14], 71), 0),
        "window_len": draw_window_len(jax.random.fold_in(splits[14], 71), 0),
    }


epsilon = 1e-05
negative_fill = -1e+30

def layer_norm(hidden, norm_gain):
    values = hidden.astype(jnp.float32)
    mean_value = lax.optimization_barrier(jnp.mean(values, axis=1, keepdims=True))
    centered = values - mean_value
    variance = lax.optimization_barrier(jnp.mean(centered * centered, axis=1, keepdims=True))
    return (centered * lax.rsqrt(variance + epsilon) * norm_gain[None, :]).astype(jnp.bfloat16)

def lookup(lookup_table, chosen):
    positions = jnp.arange(lookup_table.shape[0], dtype=jnp.int32)
    picked = jnp.where(chosen[:, None] == positions[None, :], lookup_table[None, :], 0)
    return lax.optimization_barrier(jnp.sum(picked, axis=1)).astype(jnp.int32)

def tree_rows(piece_node, mid_parent, leaf_parent, leaf_len):
    node_ids = jnp.arange(ROOTS + MIDS, dtype=jnp.int32)
    counts = lax.optimization_barrier(jnp.sum((piece_node[:, None] == node_ids[None, :]).astype(jnp.int32), axis=0))
    root_node = lookup(mid_parent, leaf_parent)
    mid_node = (leaf_parent + ROOTS).astype(jnp.int32)
    root_len = SEG * lookup(counts, root_node)
    mid_len = SEG * lookup(counts, mid_node)
    finish = root_len + mid_len + leaf_len
    return (root_node, mid_node, root_len, finish)

def piece_rank(piece_node, chosen):
    all_pieces = jnp.arange(piece_node.shape[0], dtype=jnp.int32)
    nodes_here = lookup(piece_node, chosen)
    same = (piece_node[None, :] == nodes_here[:, None]) & (all_pieces[None, :] < chosen[:, None])
    return (nodes_here, lax.optimization_barrier(jnp.sum(same.astype(jnp.int32), axis=1)))

def prefix_allowed(node_block, rank_block, root_node, mid_node, root_len, finish, sink_len, window_len):
    offsets = jnp.arange(SEG, dtype=jnp.int32)
    rel_pos = rank_block[:, None] * SEG + offsets[None, :]
    at_root = node_block[None, :] == root_node[:, None]
    at_mid = node_block[None, :] == mid_node[:, None]
    token_pos = rel_pos[None, :, :] + jnp.where(at_mid, root_len[:, None], 0)[:, :, None]
    inside = (token_pos < sink_len[:, None, None]) | (token_pos >= (finish - window_len)[:, None, None])
    return ((at_root | at_mid)[:, :, None] & inside)[:, None, :, :]

def leaf_allowed(finish, leaf_len, sink_len, window_len, leaf_max):
    offsets = jnp.arange(leaf_max, dtype=jnp.int32)
    token_pos = (finish - leaf_len)[:, None] + offsets[None, :]
    inside = (token_pos < sink_len[:, None]) | (token_pos >= (finish - window_len)[:, None])
    return (inside & (offsets[None, :] < leaf_len[:, None]))[:, None, :]

def combine(first_part, second_part):
    highest = jnp.maximum(first_part[0], second_part[0])
    factor_one = jnp.exp(first_part[0] - highest)
    factor_two = jnp.exp(second_part[0] - highest)
    totals = first_part[1] * factor_one + second_part[1] * factor_two
    summed = first_part[2] * factor_one[..., None] + second_part[2] * factor_two[..., None]
    return (highest, totals, summed)

def weigh(scores, allowed, axes):
    masked = jnp.where(allowed, scores, negative_fill)
    maxima = lax.optimization_barrier(jnp.max(masked, axis=axes))
    expanded = maxima
    for axis_pos in axes:
        expanded = jnp.expand_dims(expanded, axis_pos)
    weights = jnp.where(allowed, jnp.exp(masked - expanded), 0.0).astype(jnp.bfloat16)
    return (maxima, weights)

def reference(hidden, norm_gain, qkv_weight, out_weight, prefix_keys, prefix_values, leaf_keys, leaf_values, piece_node, mid_parent, leaf_parent, leaf_len, sink_len, window_len):
    score_scale = 1.0 / math.sqrt(HEAD_DIM)
    normed = layer_norm(hidden, norm_gain)
    flat_weight = qkv_weight.reshape(D, HEADS * 3 * HEAD_DIM)
    mixed_rows = jnp.dot(normed, flat_weight, preferred_element_type=jnp.float32).astype(jnp.bfloat16)
    mixed_rows = mixed_rows.reshape(REQUESTS, HEADS, 3, HEAD_DIM)
    query_rows = mixed_rows[:, :, 0].astype(jnp.float32)
    key_new = mixed_rows[:, :, 1].astype(jnp.float32)
    value_new = mixed_rows[:, :, 2].astype(jnp.float32)
    root_node, mid_node, root_len, finish = tree_rows(piece_node, mid_parent, leaf_parent, leaf_len)
    node_all, rank_all = piece_rank(piece_node, jnp.arange(PIECES, dtype=jnp.int32))
    blocks = PIECES // SEG_DEV

    def fold_block(carry, block_items):
        key_block, value_block, node_block, rank_block = block_items
        scores = jnp.einsum('rhd,pshd->rhps', query_rows, key_block.astype(jnp.float32)) * score_scale
        allowed = prefix_allowed(node_block, rank_block, root_node, mid_node, root_len, finish, sink_len, window_len)
        maxima, weights = weigh(scores, allowed, (2, 3))
        weights_wide = weights.astype(jnp.float32)
        totals = lax.optimization_barrier(jnp.sum(weights_wide, axis=(2, 3)))
        summed = jnp.einsum('rhps,pshd->rhd', weights_wide, value_block.astype(jnp.float32))
        return (combine(carry, (maxima, totals, summed)), None)
    start_state = (jnp.full((REQUESTS, HEADS), negative_fill, jnp.float32), jnp.zeros((REQUESTS, HEADS), jnp.float32), jnp.zeros((REQUESTS, HEADS, HEAD_DIM), jnp.float32))
    block_items = (prefix_keys.reshape(blocks, SEG_DEV, SEG, HEADS, HEAD_DIM), prefix_values.reshape(blocks, SEG_DEV, SEG, HEADS, HEAD_DIM), node_all.reshape(blocks, SEG_DEV), rank_all.reshape(blocks, SEG_DEV))
    merged, _ = lax.scan(fold_block, start_state, block_items)
    leaf_scores = jnp.einsum('rhd,rjhd->rhj', query_rows, leaf_keys.astype(jnp.float32)) * score_scale
    allowed = leaf_allowed(finish, leaf_len, sink_len, window_len, LEAF_MAX)
    leaf_max, leaf_weights = weigh(leaf_scores, allowed, (2,))
    leaf_wide = leaf_weights.astype(jnp.float32)
    leaf_part = (leaf_max, lax.optimization_barrier(jnp.sum(leaf_wide, axis=2)), jnp.einsum('rhj,rjhd->rhd', leaf_wide, leaf_values.astype(jnp.float32)))
    own_score = lax.optimization_barrier(jnp.sum(query_rows * key_new, axis=2)) * score_scale
    own_part = (own_score, jnp.ones((REQUESTS, HEADS), jnp.float32), value_new)
    merged = combine(combine(merged, leaf_part), own_part)
    attended = (merged[2] / merged[1][..., None]).astype(jnp.bfloat16).reshape(REQUESTS, HEADS * HEAD_DIM)
    return jnp.dot(attended, out_weight, preferred_element_type=jnp.float32).astype(jnp.bfloat16)
```

```python
import functools
import math

import jax
import jax.numpy as jnp
from jax import lax
from jax.experimental import pallas as pl
from jax.experimental.pallas import tpu as pltpu
from jax.sharding import PartitionSpec as P

MESH = pl.DeviceIdType.MESH
F32 = jnp.float32
BF16 = jnp.bfloat16
ROOTS = 4
EPSILON = 1e-05
NEGATIVE = -1e30
ZS = 16


def column(row):
    n = row.shape[1]
    here = lax.broadcasted_iota(jnp.int32, (n, n), 0) == lax.broadcasted_iota(jnp.int32, (n, n), 1)
    return jnp.sum(jnp.where(here, jnp.broadcast_to(row, (n, n)), 0.0), axis=1, keepdims=True)


def dot_t(a, b):
    return lax.dot_general(a, b, (((1,), (1,)), ((), ())), preferred_element_type=F32)


def dot(a, b):
    return jnp.dot(a, b, preferred_element_type=F32)


def kernel(dims, names, *refs):
    nodes, heads_n, heads, head_size, width, seg_dev, seg, leaf_max, out_width = dims
    r = dict(zip(names, refs, strict=True))
    xs = nodes // ZS
    me = lax.axis_index("nodes")
    hd = lax.axis_index("heads")
    x, z = me // ZS, lax.rem(me, ZS)
    scale = 1.0 / math.sqrt(head_size)

    def at_x(dx):
        return {"nodes": lax.rem(x + dx, xs) * ZS + z, "heads": hd}

    def far(j):
        half = (j + 1) // 2
        return lax.rem(z + ZS // 2 + half * (1 - 2 * lax.rem(j, 2)), ZS)

    def at_z(tz):
        return {"nodes": x * ZS + tz, "heads": hd}

    def at_h(dh):
        return {"nodes": me, "heads": lax.rem(hd + dh, heads_n)}

    def remote(src, dst, sem, target):
        return pltpu.make_async_remote_copy(
            src_ref=src,
            dst_ref=dst,
            send_sem=r["send"].at[sem],
            recv_sem=r["recv"].at[sem],
            device_id=target,
            device_id_type=MESH,
        )

    barrier = pltpu.get_barrier_semaphore()

    def tell(target):
        pl.semaphore_signal(barrier, inc=1, device_id=target, device_id_type=MESH)

    @pl.loop(0, ZS - 1)
    def _(j):
        tell(at_z(far(j)))

    for dx in range(1, xs):
        tell(at_x(dx))
    for dh in range(1, heads_n):
        tell(at_h(dh))

    loads = [
        pltpu.make_async_copy(r[n + "_hbm"], r[n], r["load"].at[i])
        for i, n in enumerate(("w", "k", "v", "lk", "lv", "wo"))
    ]
    for load in loads:
        load.start()

    values = r["hidden"][...].astype(F32)
    features = values.shape[1]
    mean = jnp.sum(values, axis=1, keepdims=True) * (1.0 / features)
    centered = values - mean
    variance = jnp.sum(centered * centered, axis=1, keepdims=True) * (1.0 / features)
    normed = centered * lax.rsqrt(variance + EPSILON) * r["gain"][...]
    normed = normed.astype(BF16).astype(F32)
    for n in range(nodes):
        r["rows"][n // ZS, n % ZS, :, pl.ds(0, width)] = normed[:, n * width : (n + 1) * width]

    pl.semaphore_wait(barrier, ZS - 1 + xs - 1 + heads_n - 1)

    rows, xrows, cols = r["rows"], r["xrows"], r["cols"]
    for dx in range(1, xs):
        tx = lax.rem(x + dx, xs)
        remote(rows.at[tx], xrows.at[x], 0, at_x(dx)).start()
    xrows[x] = rows[x]

    pn = r["pn"][...].astype(F32)
    pieces = pn.shape[1]
    mids = r["mp"].shape[1]
    parent = column(r["lp"][...].astype(F32))
    leaf_len = column(r["ll"][...].astype(F32))
    sink = column(r["sl"][...].astype(F32))
    window = column(r["wl"][...].astype(F32))
    mid_ids = lax.broadcasted_iota(jnp.int32, (nodes, mids), 1).astype(F32)
    mp = jnp.broadcast_to(r["mp"][...].astype(F32), (nodes, mids))
    root_node = jnp.sum(jnp.where(mid_ids == parent, mp, 0.0), axis=1, keepdims=True)
    mid_node = parent + float(ROOTS)
    pn_all = jnp.broadcast_to(pn, (nodes, pieces))
    root_len = float(seg) * jnp.sum(jnp.where(pn_all == root_node, 1.0, 0.0), axis=1, keepdims=True)
    mid_len = float(seg) * jnp.sum(jnp.where(pn_all == mid_node, 1.0, 0.0), axis=1, keepdims=True)
    finish = root_len + mid_len + leaf_len
    low = finish - window
    piece_ids = lax.broadcasted_iota(jnp.int32, (1, pieces), 1)
    offsets = lax.broadcasted_iota(jnp.int32, (nodes, seg), 1).astype(F32)
    for p in range(seg_dev):
        mine = me * seg_dev + p
        node = jnp.sum(jnp.where(piece_ids == mine, pn, 0.0), axis=1, keepdims=True)
        same = (pn == node) & (piece_ids < mine)
        rank = jnp.sum(jnp.where(same, 1.0, 0.0), axis=1, keepdims=True)
        at_mid = mid_node == node
        start = jnp.where(at_mid, root_len, 0.0) + rank * float(seg)
        position = offsets + start
        visible = ((position < sink) | (position >= low)) & (at_mid | (root_node == node))
        r["mask"][:, p * seg : (p + 1) * seg] = jnp.where(visible, 1.0, 0.0)
    my_row = lax.broadcasted_iota(jnp.int32, (nodes, 1), 0) == me

    def mine_of(values):
        return jnp.sum(jnp.where(my_row, values, 0.0), axis=0, keepdims=True)

    my_finish, my_leaf, my_sink = mine_of(finish), mine_of(leaf_len), mine_of(sink)
    my_low = mine_of(low)
    leaf_offsets = lax.broadcasted_iota(jnp.int32, (8, leaf_max), 1).astype(F32)
    leaf_position = leaf_offsets + (my_finish - my_leaf)
    leaf_visible = ((leaf_position < my_sink) | (leaf_position >= my_low)) & (leaf_offsets < my_leaf)
    r["leaf_mask"][...] = jnp.where(leaf_visible, 1.0, 0.0)

    remote(xrows.at[pl.ds(0, xs - 1)], xrows.at[pl.ds(0, xs - 1)], 0, at_x(1)).wait_recv()

    @pl.loop(0, ZS - 1)
    def _(j):
        tz = far(j)
        remote(xrows.at[:, tz], cols.at[:, z], 1, at_z(tz)).start()

    cols[:, z] = xrows[:, z]
    pq, pkv = r["pq"], r["pkv"]
    pq[:, heads, :] = jnp.zeros((nodes, head_size), F32)
    pkv[:, heads, :] = jnp.zeros((nodes, 2 * head_size), F32)
    loads[0].wait()
    some = pl.ds(0, ZS - 1)
    remote(cols.at[:, some], cols.at[:, some], 1, at_x(1)).wait_recv()

    lhs = jnp.concatenate([cols[i, :, 0, :] for i in range(xs)], axis=0)[:, :width].astype(BF16)
    for h in range(heads):
        pq[:, h, :] = dot(lhs, r["w"][h, :, pl.ds(0, head_size)])
    xq, sq, zq = r["xq"], r["sq"], r["zq"]
    for dx in range(1, xs):
        tx = lax.rem(x + dx, xs)
        remote(pq.at[pl.ds(tx * ZS, ZS)], xq.at[dx - 1], 2, at_x(dx)).start()
    for h in range(heads):
        pkv[:, h, :] = dot(lhs, r["w"][h, :, pl.ds(head_size, 2 * head_size)])
    remote(xq, xq, 2, at_x(1)).wait_recv()
    sq[...] = pq[pl.ds(x * ZS, ZS)] + xq[0] + xq[1] + xq[2]

    @pl.loop(0, ZS - 1)
    def _(j):
        tz = far(j)
        remote(sq.at[tz], zq.at[z], 3, at_z(tz)).start()

    xkv, skv, zkv = r["xkv"], r["skv"], r["zkv"]
    for dx in range(1, xs):
        tx = lax.rem(x + dx, xs)
        remote(pkv.at[pl.ds(tx * ZS, ZS)], xkv.at[dx - 1], 4, at_x(dx)).start()
    zq[z] = sq[z]
    remote(zq.at[some], zq.at[some], 3, at_x(1)).wait_recv()
    query = jnp.sum(zq[...], axis=0).astype(BF16)

    qa = r["qa"]
    qa[x, z] = query

    @pl.loop(0, ZS - 1)
    def _(j):
        remote(qa.at[x, z], qa.at[x, z], 5, at_z(far(j))).start()

    remote(xkv, xkv, 4, at_x(1)).wait_recv()
    skv[...] = pkv[pl.ds(x * ZS, ZS)] + xkv[0] + xkv[1] + xkv[2]
    remote(qa.at[0, some], qa.at[0, some], 5, at_x(1)).wait_recv()
    for dx in range(1, xs):
        remote(qa.at[x], qa.at[x], 6, at_x(dx)).start()

    @pl.loop(0, ZS - 1)
    def _(j):
        tz = far(j)
        remote(skv.at[tz], zkv.at[z], 7, at_z(tz)).start()

    zkv[z] = skv[z]

    row_ids = lax.broadcasted_iota(jnp.int32, (8, 1), 0)
    loads[3].wait()
    loads[4].wait()
    leaf_scores = jnp.zeros((8, leaf_max), F32)
    for h in range(heads):
        leaf_scores = jnp.where(row_ids == h, dot_t(query, r["lk"][h]), leaf_scores)
    leaf_on = r["leaf_mask"][...] > 0.0
    leaf_scores = jnp.where(leaf_on, leaf_scores * scale, NEGATIVE)
    leaf_m = jnp.max(leaf_scores, axis=1, keepdims=True)
    leaf_w = jnp.where(leaf_on, jnp.exp(leaf_scores - leaf_m), 0.0).astype(BF16)
    leaf_l = jnp.sum(leaf_w.astype(F32), axis=1, keepdims=True)
    leaf_n = jnp.zeros((8, head_size), F32)
    for h in range(heads):
        leaf_n = jnp.where(row_ids == h, dot(leaf_w, r["lv"][h]), leaf_n)

    loads[1].wait()
    loads[2].wait()
    three = pl.ds(0, xs - 1)
    remote(qa.at[three], qa.at[three], 6, at_x(1)).wait_recv()

    qf = r["qf"]
    qf[...] = qa[...].astype(F32).reshape(nodes, 8, head_size)
    lanes = lax.broadcasted_iota(jnp.int32, (nodes, 128), 1)
    stat_m = jnp.full((nodes, 128), NEGATIVE, F32)
    stat_l = jnp.zeros((nodes, 128), F32)
    nb, st = r["nb"], r["st"]
    for h in range(heads):
        qh = qf[:, h, :].astype(BF16)
        on = r["mask"][...] > 0.0
        scores = jnp.concatenate([dot_t(qh, r["k"][p, h]) for p in range(seg_dev)], axis=1)
        scores = jnp.where(on, scores * scale, NEGATIVE)
        top = jnp.max(scores, axis=1, keepdims=True)
        weights = jnp.where(on, jnp.exp(scores - top), 0.0).astype(BF16)
        total = jnp.sum(weights.astype(F32), axis=1, keepdims=True)
        summed = dot(weights[:, :seg], r["v"][0, h])
        for p in range(1, seg_dev):
            summed = summed + dot(weights[:, p * seg : (p + 1) * seg], r["v"][p, h])
        nb[:, h] = summed.astype(BF16).reshape(xs, ZS, head_size)
        stat_m = jnp.where(lanes == h, top, stat_m)
        stat_l = jnp.where(lanes == h, total, stat_l)
    st[:, 0] = stat_m.reshape(xs, ZS, 128)
    st[:, 1] = stat_l.reshape(xs, ZS, 128)

    xn, xst = r["xn"], r["xst"]
    for dx in range(1, xs):
        tx = lax.rem(x + dx, xs)
        remote(nb.at[tx], xn.at[dx - 1], 8, at_x(dx)).start()
        remote(st.at[tx], xst.at[dx - 1], 9, at_x(dx)).start()
    remote(xn, xn, 8, at_x(1)).wait_recv()
    remote(xst, xst, 9, at_x(1)).wait_recv()
    ms = [st[x, 0]] + [xst[i, 0] for i in range(xs - 1)]
    ls = [st[x, 1]] + [xst[i, 1] for i in range(xs - 1)]
    top = functools.reduce(jnp.maximum, ms)
    factors = [jnp.exp(m - top) for m in ms]
    total = functools.reduce(jnp.add, [f * t for f, t in zip(factors, ls, strict=True)])
    zs, zn, zn32, tn, ts = r["zs"], r["zn"], r["zn32"], r["tn"], r["ts"]
    zs[:, 0, :] = top
    zs[:, 1, :] = total
    for h in range(heads):
        parts = [nb[x, h]] + [xn[i, h] for i in range(xs - 1)]
        terms = [f[:, h : h + 1] * p.astype(F32) for f, p in zip(factors, parts, strict=True)]
        zn32[:, h, :] = functools.reduce(jnp.add, terms)
    zn32[:, heads, :] = jnp.zeros((ZS, head_size), F32)
    zn[...] = zn32[...].astype(BF16)

    @pl.loop(0, ZS - 1)
    def _(j):
        tz = far(j)
        remote(zn.at[tz], tn.at[z], 10, at_z(tz)).start()
        remote(zs.at[tz], ts.at[z], 11, at_z(tz)).start()

    tn[z] = zn[z]
    ts[z] = zs[z]

    remote(zkv.at[some], zkv.at[some], 7, at_x(1)).wait_recv()
    new = jnp.sum(zkv[...], axis=0).astype(BF16).astype(F32)
    own_m = jnp.sum(query.astype(F32) * new[:, :head_size], axis=1, keepdims=True) * scale
    own_n = new[:, head_size:]

    remote(tn.at[some], tn.at[some], 10, at_x(1)).wait_recv()
    remote(ts.at[some], ts.at[some], 11, at_x(1)).wait_recv()
    diagonal = lax.broadcasted_iota(jnp.int32, (8, 128), 0) == lax.broadcasted_iota(
        jnp.int32, (8, 128), 1
    )

    def stat(i, which):
        row = jnp.broadcast_to(ts[i, which : which + 1, :], (8, 128))
        return jnp.sum(jnp.where(diagonal, row, 0.0), axis=1, keepdims=True)

    ms = [stat(i, 0) for i in range(ZS)]
    top = functools.reduce(jnp.maximum, ms + [leaf_m, own_m])
    own_f = jnp.exp(own_m - top)
    leaf_f = jnp.exp(leaf_m - top)
    total = own_f + leaf_f * leaf_l
    summed = own_f * own_n + leaf_f * leaf_n
    for i in range(ZS):
        f = jnp.exp(ms[i] - top)
        total = total + f * stat(i, 1)
        summed = summed + f * tn[i].astype(F32)
    attended = (summed / total).astype(BF16)

    aa = r["aa"]
    aa[x, z] = attended

    @pl.loop(0, ZS - 1)
    def _(j):
        remote(aa.at[x, z], aa.at[x, z], 12, at_z(far(j))).start()

    loads[5].wait()
    remote(aa.at[0, some], aa.at[0, some], 12, at_x(1)).wait_recv()
    for dx in range(1, xs):
        remote(aa.at[x], aa.at[x], 13, at_x(dx)).start()
    remote(aa.at[three], aa.at[three], 13, at_x(1)).wait_recv()

    qf[...] = aa[...].astype(F32).reshape(nodes, 8, head_size)
    acc = jnp.zeros((nodes, out_width), F32)
    for h in range(heads):
        acc = acc + dot_t(qf[:, h, :].astype(BF16), r["wo"][:, h * head_size : (h + 1) * head_size])
    rows_out = nodes // heads_n
    os, orr = r["os"], r["orr"]
    os[:, :, pl.ds(0, out_width)] = acc.reshape(heads_n, rows_out, out_width)
    for dh in range(1, heads_n):
        remote(os.at[lax.rem(hd + dh, heads_n)], orr.at[dh - 1], 14, at_h(dh)).start()
    remote(orr, orr, 14, at_x(1)).wait_recv()
    result = os[hd] + jnp.sum(orr[...], axis=0)
    r["out"][...] = result[:, :out_width].astype(BF16)

    for sem, ref in (
        (0, xrows.at[three]),
        (1, cols.at[:, some]),
        (2, xq),
        (3, zq.at[some]),
        (4, xkv),
        (5, qa.at[0, some]),
        (6, qa.at[three]),
        (7, zkv.at[some]),
        (8, xn),
        (9, xst),
        (10, tn.at[some]),
        (11, ts.at[some]),
        (12, aa.at[0, some]),
        (13, aa.at[three]),
        (14, orr),
    ):
        remote(ref, ref, sem, at_x(1)).wait_send()


def on_device(
    hidden,
    norm_gain,
    qkv_weight,
    out_weight,
    prefix_keys,
    prefix_values,
    leaf_keys,
    leaf_values,
    piece_node,
    mid_parent,
    leaf_parent,
    leaf_len,
    sink_len,
    window_len,
):
    nodes = lax.axis_size("nodes")
    heads_n = lax.axis_size("heads")
    xs = nodes // ZS
    width, heads, triple = qkv_weight.shape
    head_size = triple // 3
    seg_dev, seg = prefix_keys.shape[:2]
    leaf_max = leaf_keys.shape[1]
    out_width = out_weight.shape[1]
    rows_out = nodes // heads_n
    dims = (nodes, heads_n, heads, head_size, width, seg_dev, seg, leaf_max, out_width)
    small = {
        "hidden": hidden,
        "gain": norm_gain[None, :],
        "pn": piece_node[None, :],
        "mp": mid_parent[None, :],
        "lp": leaf_parent[None, :],
        "ll": leaf_len[None, :],
        "sl": sink_len[None, :],
        "wl": window_len[None, :],
    }
    large = {
        "w_hbm": qkv_weight.transpose(1, 0, 2),
        "wo_hbm": out_weight.T,
        "k_hbm": prefix_keys.transpose(0, 2, 1, 3),
        "v_hbm": prefix_values.transpose(0, 2, 1, 3),
        "lk_hbm": leaf_keys[0].transpose(1, 0, 2),
        "lv_hbm": leaf_values[0].transpose(1, 0, 2),
    }
    vmem = pltpu.VMEM
    scratch = {n[:-4]: vmem(a.shape, a.dtype) for n, a in large.items()}
    scratch |= {
        "rows": vmem((xs, ZS, 1, 128), F32),
        "xrows": vmem((xs, ZS, 1, 128), F32),
        "cols": vmem((xs, ZS, 1, 128), F32),
        "mask": vmem((nodes, seg_dev * seg), F32),
        "leaf_mask": vmem((8, leaf_max), F32),
        "pq": vmem((nodes, 8, head_size), F32),
        "xq": vmem((xs - 1, ZS, 8, head_size), F32),
        "sq": vmem((ZS, 8, head_size), F32),
        "zq": vmem((ZS, 8, head_size), F32),
        "pkv": vmem((nodes, 8, 2 * head_size), F32),
        "xkv": vmem((xs - 1, ZS, 8, 2 * head_size), F32),
        "skv": vmem((ZS, 8, 2 * head_size), F32),
        "zkv": vmem((ZS, 8, 2 * head_size), F32),
        "qa": vmem((xs, ZS, 8, head_size), BF16),
        "aa": vmem((xs, ZS, 8, head_size), BF16),
        "qf": vmem((nodes, 8, head_size), F32),
        "nb": vmem((xs, heads, ZS, head_size), BF16),
        "xn": vmem((xs - 1, heads, ZS, head_size), BF16),
        "st": vmem((xs, 2, ZS, 128), F32),
        "xst": vmem((xs - 1, 2, ZS, 128), F32),
        "zn32": vmem((ZS, 8, head_size), F32),
        "zn": vmem((ZS, 8, head_size), BF16),
        "tn": vmem((ZS, 8, head_size), BF16),
        "zs": vmem((ZS, 2, 128), F32),
        "ts": vmem((ZS, 2, 128), F32),
        "os": vmem((heads_n, rows_out, 128), F32),
        "orr": vmem((heads_n - 1, rows_out, 128), F32),
        "load": pltpu.SemaphoreType.DMA((6,)),
        "send": pltpu.SemaphoreType.DMA((15,)),
        "recv": pltpu.SemaphoreType.DMA((15,)),
    }
    names = list(small) + list(large) + ["out"] + list(scratch)
    return pl.pallas_call(
        functools.partial(kernel, dims, names),
        out_shape=jax.ShapeDtypeStruct((rows_out, out_width), BF16),
        in_specs=[pl.BlockSpec(memory_space=pltpu.VMEM)] * len(small)
        + [pl.BlockSpec(memory_space=pl.ANY)] * len(large),
        out_specs=pl.BlockSpec(memory_space=pltpu.VMEM),
        scratch_shapes=list(scratch.values()),
        compiler_params=pltpu.CompilerParams(
            collective_id=0, has_side_effects=True, vmem_limit_bytes=60 * 2**20
        ),
    )(*small.values(), *large.values())


def solution(mesh):
    return jax.shard_map(
        on_device,
        mesh=mesh,
        in_specs=(
            P("nodes", None),
            P(),
            P("nodes", "heads", None),
            P("heads", "nodes"),
            P("nodes", None, "heads", None),
            P("nodes", None, "heads", None),
            P("nodes", None, "heads", None),
            P("nodes", None, "heads", None),
            P(),
            P(),
            P(),
            P(),
            P(),
            P(),
        ),
        out_specs=P("heads", "nodes"),
        check_vma=False,
    )
```

```python
import functools
import math

import jax
import jax.numpy as jnp
from jax import lax
from jax.experimental import pallas as pl
from jax.experimental.pallas import tpu as pltpu
from jax.sharding import PartitionSpec as P

MESH = pl.DeviceIdType.MESH
F32 = jnp.float32
BF16 = jnp.bfloat16
ROOTS = 4
EPSILON = 1e-05
NEGATIVE = -1e30
LOADED = ("hidden", "gain", "pn", "mp", "lp", "ll", "sl", "wl", "w", "k", "v", "lk", "lv", "wo")
ZS = 16


def rho(n):
    z = lax.rem(n, ZS) if not isinstance(n, int) else n % ZS
    return n - z + (z % 4) * 4 + z // 4


def column(row):
    n = row.shape[1]
    i = lax.broadcasted_iota(jnp.int32, (n, n), 0)
    here = (i // ZS) * ZS + (i % 4) * 4 + (i % ZS) // 4 == lax.broadcasted_iota(jnp.int32, (n, n), 1)
    return jnp.sum(jnp.where(here, jnp.broadcast_to(row, (n, n)), 0.0), axis=1, keepdims=True)


def dot_t(a, b):
    return lax.dot_general(a, b, (((1,), (1,)), ((), ())), preferred_element_type=F32)


def dot(a, b):
    return jnp.dot(a, b, preferred_element_type=F32)


def kernel(dims, names, *refs):
    nodes, heads_n, heads, head_size, width, seg_dev, seg, leaf_max, out_width = dims
    r = dict(zip(names, refs, strict=True))
    xs = nodes // ZS
    me = lax.axis_index("nodes")
    hd = lax.axis_index("heads")
    x, z = me // ZS, lax.rem(me, ZS)
    mine, block, turn = rho(me), x * 4 + lax.rem(z, 4), z // 4
    scale = 1.0 / math.sqrt(head_size)
    near = xs * 4 - 1
    owned = pl.ds(block * 4, 4)

    def at(tx, tz):
        return {"nodes": tx * ZS + tz, "heads": hd}

    def far(j):
        half = (j + 1) // 2
        return lax.rem(z + ZS // 2 + half * (1 - 2 * lax.rem(j, 2)), ZS)

    def across(j):
        return lax.rem(x + j, xs)

    def neighbour(j):
        i, k = lax.rem(j, 4), j // 4
        dx = 2 + ((i + 1) // 2) * (1 - 2 * lax.rem(i, 2))
        dz = 2 - k - k // 2 + 2 * (k // 3)
        return lax.rem(x + dx, xs), lax.rem(z + dz + ZS, ZS)

    def remote(src, dst, sem, target):
        return pltpu.make_async_remote_copy(
            src_ref=src,
            dst_ref=dst,
            send_sem=r["send"].at[sem],
            recv_sem=r["recv"].at[sem],
            device_id=target,
            device_id_type=MESH,
        )

    other = at(across(1), z)
    sent = []

    def arrive(sem, ref):
        remote(ref, ref, sem, other).wait_recv()
        sent.append((sem, ref))

    loads = {
        n: pltpu.make_async_copy(r[n + "_hbm"], r[n], r["load"].at[i])
        for i, n in enumerate(LOADED)
    }
    loads["hidden"].start()
    loads["gain"].start()
    barrier = pltpu.get_barrier_semaphore()

    def tell(target):
        pl.semaphore_signal(barrier, inc=1, device_id=target, device_id_type=MESH)

    @pl.loop(0, ZS - 1)
    def _(j):
        for dx in (2, 1, 3, 0):
            tell(at(across(dx), far(j)))

    for dx in range(1, xs):
        tell(at(across(dx), z))
    for dh in range(1, heads_n):
        tell({"nodes": me, "heads": lax.rem(hd + dh, heads_n)})

    for n in LOADED[2:]:
        loads[n].start()

    loads["hidden"].wait()
    loads["gain"].wait()
    values = r["hidden"][...].astype(F32)
    features = values.shape[1]
    mean = jnp.sum(values, axis=1, keepdims=True) * (1.0 / features)
    centered = values - mean
    variance = jnp.sum(centered * centered, axis=1, keepdims=True) * (1.0 / features)
    normed = centered * lax.rsqrt(variance + EPSILON) * r["gain"][...]
    normed = normed.astype(BF16).astype(F32)
    rows, cols = r["rows"], r["cols"]
    for n in range(nodes):
        rows[n, :, pl.ds(0, width)] = normed[:, n * width : (n + 1) * width]

    pl.semaphore_wait(barrier, nodes - 1 + heads_n - 1)

    @pl.loop(0, ZS - 1)
    def _(j):
        tz = far(j)
        for dx in (2, 1, 3, 0):
            tx = across(dx)
            remote(rows.at[tx * ZS + tz], cols.at[mine], 0, at(tx, tz)).start()

    for dx in range(1, xs):
        tx = across(dx)
        remote(rows.at[tx * ZS + z], cols.at[mine], 0, at(tx, z)).start()
    cols[mine] = rows[me]

    for n in ("pn", "mp", "lp", "ll", "sl", "wl"):
        loads[n].wait()
    pn = r["pn"][...].astype(F32)
    pieces = pn.shape[1]
    mids = r["mp"].shape[1]
    parent = column(r["lp"][...].astype(F32))
    leaf_len = column(r["ll"][...].astype(F32))
    sink = column(r["sl"][...].astype(F32))
    window = column(r["wl"][...].astype(F32))
    mid_ids = lax.broadcasted_iota(jnp.int32, (nodes, mids), 1).astype(F32)
    mp = jnp.broadcast_to(r["mp"][...].astype(F32), (nodes, mids))
    root_node = jnp.sum(jnp.where(mid_ids == parent, mp, 0.0), axis=1, keepdims=True)
    mid_node = parent + float(ROOTS)
    pn_all = jnp.broadcast_to(pn, (nodes, pieces))
    root_len = float(seg) * jnp.sum(jnp.where(pn_all == root_node, 1.0, 0.0), axis=1, keepdims=True)
    mid_len = float(seg) * jnp.sum(jnp.where(pn_all == mid_node, 1.0, 0.0), axis=1, keepdims=True)
    finish = root_len + mid_len + leaf_len
    low = finish - window
    piece_ids = lax.broadcasted_iota(jnp.int32, (1, pieces), 1)
    offsets = lax.broadcasted_iota(jnp.int32, (nodes, seg), 1).astype(F32)
    for p in range(seg_dev):
        here = me * seg_dev + p
        node = jnp.sum(jnp.where(piece_ids == here, pn, 0.0), axis=1, keepdims=True)
        same = (pn == node) & (piece_ids < here)
        rank = jnp.sum(jnp.where(same, 1.0, 0.0), axis=1, keepdims=True)
        at_mid = mid_node == node
        start = jnp.where(at_mid, root_len, 0.0) + rank * float(seg)
        position = offsets + start
        visible = ((position < sink) | (position >= low)) & (at_mid | (root_node == node))
        r["mask"][:, p * seg : (p + 1) * seg] = jnp.where(visible, 1.0, 0.0)
    my_row = lax.broadcasted_iota(jnp.int32, (nodes, 1), 0) == mine

    def mine_of(values):
        return jnp.sum(jnp.where(my_row, values, 0.0), axis=0, keepdims=True)

    my_finish, my_leaf, my_sink = mine_of(finish), mine_of(leaf_len), mine_of(sink)
    my_low = mine_of(low)
    leaf_offsets = lax.broadcasted_iota(jnp.int32, (8, leaf_max), 1).astype(F32)
    leaf_position = leaf_offsets + (my_finish - my_leaf)
    leaf_visible = ((leaf_position < my_sink) | (leaf_position >= my_low)) & (leaf_offsets < my_leaf)
    r["leaf_mask"][...] = jnp.where(leaf_visible, 1.0, 0.0)

    pq, pkv = r["pq"], r["pkv"]
    pq[:, heads, :] = jnp.zeros((nodes, head_size), F32)
    pkv[:, heads, :] = jnp.zeros((nodes, 2 * head_size), F32)
    loads["w"].wait()
    arrive(0, cols.at[pl.ds(0, nodes - 1)])

    lhs = cols[:, 0, :][:, :width].astype(BF16)
    for h in range(heads):
        pq[:, h, :] = dot(lhs, r["w"][h, :, pl.ds(0, head_size)])
    nq, fq = r["nq"], r["fq"]

    @pl.loop(0, near)
    def _(j):
        tx, tz = neighbour(j)
        src = pq.at[pl.ds((tx * 4 + lax.rem(tz, 4)) * 4, 4)]
        remote(src, nq.at[j], 1, at(tx, tz)).start()

    for h in range(heads):
        pkv[:, h, :] = dot(lhs, r["w"][h, :, pl.ds(head_size, 2 * head_size)])
    arrive(1, nq)
    fq[turn] = pq[owned] + jnp.sum(nq[...], axis=0)
    distant = [lax.rem(z + 4 * d, ZS) for d in (2, 1, 3)]
    for tz in distant:
        remote(fq.at[turn], fq.at[turn], 2, at(x, tz)).start()

    xkv, skv, nkv, tkv, fkv = r["xkv"], r["skv"], r["nkv"], r["tkv"], r["fkv"]
    for dx in range(1, xs):
        tx = across(dx)
        remote(pkv.at[pl.ds(tx * ZS, ZS)], xkv.at[dx - 1], 3, at(tx, z)).start()
    three = pl.ds(0, 3)
    arrive(2, fq.at[three])

    qa = r["qa"]
    qa[owned] = jnp.sum(fq[...], axis=0).astype(BF16)

    @pl.loop(0, near)
    def _(j):
        tx, tz = neighbour(j)
        remote(qa.at[owned], qa.at[owned], 4, at(tx, tz)).start()

    arrive(3, xkv)
    skv[...] = pkv[pl.ds(x * ZS, ZS)] + jnp.sum(xkv[...], axis=0)
    for i, dz in enumerate((2, 1, -1)):
        tz = lax.rem(z + dz + ZS, ZS)
        remote(skv.at[pl.ds(lax.rem(tz, 4) * 4, 4)], nkv.at[i], 5, at(x, tz)).start()

    query = qa[mine]
    row_ids = lax.broadcasted_iota(jnp.int32, (8, 1), 0)
    loads["lk"].wait()
    loads["lv"].wait()
    leaf_scores = jnp.zeros((8, leaf_max), F32)
    for h in range(heads):
        leaf_scores = jnp.where(row_ids == h, dot_t(query, r["lk"][h]), leaf_scores)
    leaf_on = r["leaf_mask"][...] > 0.0
    leaf_scores = jnp.where(leaf_on, leaf_scores * scale, NEGATIVE)
    leaf_m = jnp.max(leaf_scores, axis=1, keepdims=True)
    leaf_w = jnp.where(leaf_on, jnp.exp(leaf_scores - leaf_m), 0.0).astype(BF16)
    leaf_l = jnp.sum(leaf_w.astype(F32), axis=1, keepdims=True)
    leaf_n = jnp.zeros((8, head_size), F32)
    for h in range(heads):
        leaf_n = jnp.where(row_ids == h, dot(leaf_w, r["lv"][h]), leaf_n)

    arrive(5, nkv)
    tkv[...] = skv[pl.ds(lax.rem(z, 4) * 4, 4)] + jnp.sum(nkv[...], axis=0)
    for i, tz in enumerate(distant):
        remote(tkv.at[tz // 4], fkv.at[i], 6, at(x, tz)).start()
    loads["k"].wait()
    loads["v"].wait()
    arrive(4, qa.at[pl.ds(0, near * 4)])

    qf = r["qf"]
    qf[...] = qa[...].astype(F32)
    lanes = lax.broadcasted_iota(jnp.int32, (nodes, 128), 1)
    stat_m = jnp.full((nodes, 128), NEGATIVE, F32)
    stat_l = jnp.zeros((nodes, 128), F32)
    nb32, nb, st = r["nb32"], r["nb"], r["st"]
    for h in range(heads):
        qh = qf[:, h, :].astype(BF16)
        on = r["mask"][...] > 0.0
        scores = jnp.concatenate([dot_t(qh, r["k"][p, h]) for p in range(seg_dev)], axis=1)
        scores = jnp.where(on, scores * scale, NEGATIVE)
        top = jnp.max(scores, axis=1, keepdims=True)
        weights = jnp.where(on, jnp.exp(scores - top), 0.0).astype(BF16)
        total = jnp.sum(weights.astype(F32), axis=1, keepdims=True)
        summed = dot(weights[:, :seg], r["v"][0, h])
        for p in range(1, seg_dev):
            summed = summed + dot(weights[:, p * seg : (p + 1) * seg], r["v"][p, h])
        nb32[:, h, :] = summed
        stat_m = jnp.where(lanes == h, top, stat_m)
        stat_l = jnp.where(lanes == h, total, stat_l)
    nb32[:, heads, :] = jnp.zeros((nodes, head_size), F32)
    nb[...] = nb32[...].astype(BF16)
    st[:, 0, :] = stat_m
    st[:, 1, :] = stat_l

    xn, xst, fn, fs = r["xn"], r["xst"], r["fn"], r["fs"]

    @pl.loop(0, near)
    def _(j):
        tx, tz = neighbour(j)
        there = pl.ds((tx * 4 + lax.rem(tz, 4)) * 4, 4)
        remote(st.at[there], xst.at[j], 7, at(tx, tz)).start()
        remote(nb.at[there], xn.at[j], 8, at(tx, tz)).start()

    xst[near] = st[owned]
    xn[near] = nb[owned]
    diagonal = lax.broadcasted_iota(jnp.int32, (8, 128), 0) == lax.broadcasted_iota(
        jnp.int32, (8, 128), 1
    )

    def upright(row):
        spread = jnp.broadcast_to(row, (8, 128))
        return jnp.sum(jnp.where(diagonal, spread, 0.0), axis=1, keepdims=True)

    def flat(col, rest):
        spread = jnp.sum(jnp.where(diagonal, jnp.broadcast_to(col, (8, 128)), 0.0), axis=0, keepdims=True)
        return jnp.where(lax.broadcasted_iota(jnp.int32, (1, 128), 1) < 8, spread, rest)

    arrive(6, fkv)
    new = (tkv[turn] + jnp.sum(fkv[...], axis=0)).astype(BF16).astype(F32)
    own_m = jnp.sum(query.astype(F32) * new[:, :head_size], axis=1, keepdims=True) * scale
    extra_m = jnp.maximum(own_m, leaf_m)
    own_f, leaf_f = jnp.exp(own_m - extra_m), jnp.exp(leaf_m - extra_m)
    extra_l = own_f + leaf_f * leaf_l
    extra_n = own_f * new[:, head_size:] + leaf_f * leaf_n
    is_mine = lax.broadcasted_iota(jnp.int32, (4, 1), 0) == turn
    extra_ms = jnp.where(is_mine, flat(extra_m, NEGATIVE), NEGATIVE)
    extra_ls = jnp.where(is_mine, flat(extra_l, 0.0), 0.0)

    arrive(7, xst.at[pl.ds(0, near)])
    ms = xst[:, :, 0, :]
    top = jnp.maximum(jnp.max(ms, axis=0), extra_ms)
    factors = jnp.exp(ms - top[None])
    extra_f = jnp.where(is_mine, jnp.exp(extra_ms - top), 0.0)
    total = jnp.sum(factors * xst[:, :, 1, :], axis=0) + extra_f * extra_ls
    fs[turn, :, 0, :] = top
    fs[turn, :, 1, :] = total
    for tz in distant:
        remote(fs.at[turn], fs.at[turn], 9, at(x, tz)).start()
    arrive(8, xn.at[pl.ds(0, near)])
    for i in range(4):
        summed = upright(extra_f[i : i + 1]) * extra_n
        for s in range(near + 1):
            summed = summed + upright(factors[s, i : i + 1]) * xn[s, i].astype(F32)
        fn[turn, i] = summed.astype(BF16)
    for tz in distant:
        remote(fn.at[turn], fn.at[turn], 10, at(x, tz)).start()
    arrive(9, fs.at[three])
    ms = fs[:, :, 0, :]
    top = jnp.max(ms, axis=0)
    factors = jnp.exp(ms - top[None])
    total = jnp.sum(factors * fs[:, :, 1, :], axis=0)
    total = jnp.where(lax.broadcasted_iota(jnp.int32, (4, 128), 1) < heads, total, 1.0)
    factors = factors / total[None]
    factors = [[upright(factors[s, i : i + 1]) for s in range(4)] for i in range(4)]
    arrive(10, fn.at[three])

    aa = r["aa"]
    for i in range(4):
        attended = sum(factors[i][s] * fn[s, i].astype(F32) for s in range(4))
        aa[block * 4 + i] = attended.astype(BF16)

    @pl.loop(0, near)
    def _(j):
        tx, tz = neighbour(j)
        remote(aa.at[owned], aa.at[owned], 11, at(tx, tz)).start()

    loads["wo"].wait()
    arrive(11, aa.at[pl.ds(0, near * 4)])

    for n in range(nodes):
        qf[n] = aa[rho(n)].astype(F32)
    acc = jnp.zeros((nodes, out_width), F32)
    for h in range(heads):
        acc = acc + dot_t(qf[:, h, :].astype(BF16), r["wo"][:, h * head_size : (h + 1) * head_size])
    rows_out = nodes // heads_n
    os, orr = r["os"], r["orr"]
    os[:, :, pl.ds(0, out_width)] = acc.reshape(heads_n, rows_out, out_width)
    for dh in range(1, heads_n):
        th = lax.rem(hd + dh, heads_n)
        remote(os.at[th], orr.at[dh - 1], 12, {"nodes": me, "heads": th}).start()
    arrive(12, orr)
    result = os[hd] + jnp.sum(orr[...], axis=0)
    r["out"][...] = result[:, :out_width].astype(BF16)

    for sem, ref in sent:
        remote(ref, ref, sem, other).wait_send()


def on_device(
    hidden,
    norm_gain,
    qkv_weight,
    out_weight,
    prefix_keys,
    prefix_values,
    leaf_keys,
    leaf_values,
    piece_node,
    mid_parent,
    leaf_parent,
    leaf_len,
    sink_len,
    window_len,
):
    nodes = lax.axis_size("nodes")
    heads_n = lax.axis_size("heads")
    xs = nodes // ZS
    width, heads, triple = qkv_weight.shape
    head_size = triple // 3
    seg_dev, seg = prefix_keys.shape[:2]
    leaf_max = leaf_keys.shape[1]
    out_width = out_weight.shape[1]
    rows_out = nodes // heads_n
    dims = (nodes, heads_n, heads, head_size, width, seg_dev, seg, leaf_max, out_width)
    large = {
        "hidden_hbm": hidden,
        "gain_hbm": norm_gain[None, :],
        "pn_hbm": piece_node[None, :],
        "mp_hbm": mid_parent[None, :],
        "lp_hbm": leaf_parent[None, :],
        "ll_hbm": leaf_len[None, :],
        "sl_hbm": sink_len[None, :],
        "wl_hbm": window_len[None, :],
        "w_hbm": qkv_weight.transpose(1, 0, 2),
        "wo_hbm": out_weight.T,
        "k_hbm": prefix_keys.transpose(0, 2, 1, 3),
        "v_hbm": prefix_values.transpose(0, 2, 1, 3),
        "lk_hbm": leaf_keys[0].transpose(1, 0, 2),
        "lv_hbm": leaf_values[0].transpose(1, 0, 2),
    }
    vmem = pltpu.VMEM
    scratch = {n[:-4]: vmem(a.shape, a.dtype) for n, a in large.items()}
    scratch |= {
        "rows": vmem((nodes, 1, 128), F32),
        "cols": vmem((nodes, 1, 128), F32),
        "mask": vmem((nodes, seg_dev * seg), F32),
        "leaf_mask": vmem((8, leaf_max), F32),
        "pq": vmem((nodes, 8, head_size), F32),
        "nq": vmem((xs * 4 - 1, 4, 8, head_size), F32),
        "fq": vmem((4, 4, 8, head_size), F32),
        "pkv": vmem((nodes, 8, 2 * head_size), F32),
        "xkv": vmem((xs - 1, ZS, 8, 2 * head_size), F32),
        "skv": vmem((ZS, 8, 2 * head_size), F32),
        "nkv": vmem((3, 4, 8, 2 * head_size), F32),
        "tkv": vmem((4, 8, 2 * head_size), F32),
        "fkv": vmem((3, 8, 2 * head_size), F32),
        "qa": vmem((nodes, 8, head_size), BF16),
        "aa": vmem((nodes, 8, head_size), BF16),
        "qf": vmem((nodes, 8, head_size), F32),
        "nb32": vmem((nodes, 8, head_size), F32),
        "nb": vmem((nodes, 8, head_size), BF16),
        "xn": vmem((xs * 4, 4, 8, head_size), BF16),
        "st": vmem((nodes, 2, 128), F32),
        "xst": vmem((xs * 4, 4, 2, 128), F32),
        "fn": vmem((4, 4, 8, head_size), BF16),
        "fs": vmem((4, 4, 2, 128), F32),
        "os": vmem((heads_n, rows_out, 128), F32),
        "orr": vmem((heads_n - 1, rows_out, 128), F32),
        "load": pltpu.SemaphoreType.DMA((len(LOADED),)),
        "send": pltpu.SemaphoreType.DMA((13,)),
        "recv": pltpu.SemaphoreType.DMA((13,)),
    }
    names = list(large) + ["out"] + list(scratch)
    return pl.pallas_call(
        functools.partial(kernel, dims, names),
        out_shape=jax.ShapeDtypeStruct((rows_out, out_width), BF16),
        in_specs=[pl.BlockSpec(memory_space=pl.ANY)] * len(large),
        out_specs=pl.BlockSpec(memory_space=pltpu.VMEM),
        scratch_shapes=list(scratch.values()),
        compiler_params=pltpu.CompilerParams(
            collective_id=0, has_side_effects=True, vmem_limit_bytes=60 * 2**20
        ),
    )(*large.values())


def solution(mesh):
    return jax.shard_map(
        on_device,
        mesh=mesh,
        in_specs=(
            P("nodes", None),
            P(),
            P("nodes", "heads", None),
            P("heads", "nodes"),
            P("nodes", None, "heads", None),
            P("nodes", None, "heads", None),
            P("nodes", None, "heads", None),
            P("nodes", None, "heads", None),
            P(),
            P(),
            P(),
            P(),
            P(),
            P(),
        ),
        out_specs=P("heads", "nodes"),
        check_vma=False,
    )
```

```python
import functools
import math

import jax
import jax.numpy as jnp
from jax import lax
from jax.experimental import pallas as pl
from jax.experimental.pallas import tpu as pltpu
from jax.sharding import PartitionSpec as P

MESH = pl.DeviceIdType.MESH
F32 = jnp.float32
BF16 = jnp.bfloat16
ROOTS = 4
EPSILON = 1e-05
NEGATIVE = -1e30
LOADED = ("hidden", "gain", "pn", "mp", "lp", "ll", "sl", "wl", "w", "k", "v", "lk", "lv", "wo")
ZS = 16


def rho(n):
    z = lax.rem(n, ZS) if not isinstance(n, int) else n % ZS
    return n - z + (z % 4) * 4 + z // 4


def column(row):
    n = row.shape[1]
    i = lax.broadcasted_iota(jnp.int32, (n, n), 0)
    here = (i // ZS) * ZS + (i % 4) * 4 + (i % ZS) // 4 == lax.broadcasted_iota(jnp.int32, (n, n), 1)
    return jnp.sum(jnp.where(here, jnp.broadcast_to(row, (n, n)), 0.0), axis=1, keepdims=True)


def dot_t(a, b):
    return lax.dot_general(a, b, (((1,), (1,)), ((), ())), preferred_element_type=F32)


def dot(a, b):
    return jnp.dot(a, b, preferred_element_type=F32)


def kernel(dims, names, *refs):
    nodes, heads_n, heads, head_size, width, seg_dev, seg, leaf_max, out_width = dims
    r = dict(zip(names, refs, strict=True))
    xs = nodes // ZS
    me = lax.axis_index("nodes")
    hd = lax.axis_index("heads")
    x, z = me // ZS, lax.rem(me, ZS)
    mine, block, turn = rho(me), x * 4 + lax.rem(z, 4), z // 4
    scale = 1.0 / math.sqrt(head_size)
    near = xs * 4 - 1
    owned = pl.ds(block * 4, 4)

    def at(tx, tz):
        return {"nodes": tx * ZS + tz, "heads": hd}

    def far(j):
        half = (j + 1) // 2
        return lax.rem(z + ZS // 2 + half * (1 - 2 * lax.rem(j, 2)), ZS)

    def across(j):
        return lax.rem(x + j, xs)

    def neighbour(j):
        i, k = lax.rem(j, 4), j // 4
        dx = 2 + ((i + 1) // 2) * (1 - 2 * lax.rem(i, 2))
        dz = 2 - k - k // 2 + 2 * (k // 3)
        return lax.rem(x + dx, xs), lax.rem(z + dz + ZS, ZS)

    def remote(src, dst, sem, target):
        return pltpu.make_async_remote_copy(
            src_ref=src,
            dst_ref=dst,
            send_sem=r["send"].at[sem],
            recv_sem=r["recv"].at[sem],
            device_id=target,
            device_id_type=MESH,
        )

    other = at(across(1), z)
    sent = []

    def arrive(sem, ref):
        remote(ref, ref, sem, other).wait_recv()
        sent.append((sem, ref))

    loads = {
        n: pltpu.make_async_copy(r[n + "_hbm"], r[n], r["load"].at[i])
        for i, n in enumerate(LOADED)
    }
    loads["hidden"].start()
    loads["gain"].start()
    barrier = pltpu.get_barrier_semaphore()

    def tell(target):
        pl.semaphore_signal(barrier, inc=1, device_id=target, device_id_type=MESH)

    @pl.loop(0, ZS - 1)
    def _(j):
        for dx in (2, 1, 3, 0):
            tell(at(across(dx), far(j)))

    for dx in range(1, xs):
        tell(at(across(dx), z))
    for dh in range(1, heads_n):
        tell({"nodes": me, "heads": lax.rem(hd + dh, heads_n)})

    for n in LOADED[2:]:
        loads[n].start()

    loads["hidden"].wait()
    loads["gain"].wait()
    values = r["hidden"][...].astype(F32)
    features = values.shape[1]
    mean = jnp.sum(values, axis=1, keepdims=True) * (1.0 / features)
    centered = values - mean
    variance = jnp.sum(centered * centered, axis=1, keepdims=True) * (1.0 / features)
    normed = centered * lax.rsqrt(variance + EPSILON) * r["gain"][...]
    normed = normed.astype(BF16).astype(F32)
    rows, cols = r["rows"], r["cols"]
    for n in range(nodes):
        rows[n, :, pl.ds(0, width)] = normed[:, n * width : (n + 1) * width]

    pl.semaphore_wait(barrier, nodes - 1 + heads_n - 1)

    @pl.loop(0, ZS - 1)
    def _(j):
        tz = far(j)
        for dx in (2, 1, 3, 0):
            tx = across(dx)
            remote(rows.at[tx * ZS + tz], cols.at[mine], 0, at(tx, tz)).start()

    for dx in range(1, xs):
        tx = across(dx)
        remote(rows.at[tx * ZS + z], cols.at[mine], 0, at(tx, z)).start()
    cols[mine] = rows[me]

    for n in ("pn", "mp", "lp", "ll", "sl", "wl"):
        loads[n].wait()
    pn = r["pn"][...].astype(F32)
    pieces = pn.shape[1]
    mids = r["mp"].shape[1]
    parent = column(r["lp"][...].astype(F32))
    leaf_len = column(r["ll"][...].astype(F32))
    sink = column(r["sl"][...].astype(F32))
    window = column(r["wl"][...].astype(F32))
    mid_ids = lax.broadcasted_iota(jnp.int32, (nodes, mids), 1).astype(F32)
    mp = jnp.broadcast_to(r["mp"][...].astype(F32), (nodes, mids))
    root_node = jnp.sum(jnp.where(mid_ids == parent, mp, 0.0), axis=1, keepdims=True)
    mid_node = parent + float(ROOTS)
    pn_all = jnp.broadcast_to(pn, (nodes, pieces))
    root_len = float(seg) * jnp.sum(jnp.where(pn_all == root_node, 1.0, 0.0), axis=1, keepdims=True)
    mid_len = float(seg) * jnp.sum(jnp.where(pn_all == mid_node, 1.0, 0.0), axis=1, keepdims=True)
    finish = root_len + mid_len + leaf_len
    low = finish - window
    piece_ids = lax.broadcasted_iota(jnp.int32, (1, pieces), 1)
    offsets = lax.broadcasted_iota(jnp.int32, (nodes, seg), 1).astype(F32)
    for p in range(seg_dev):
        here = me * seg_dev + p
        node = jnp.sum(jnp.where(piece_ids == here, pn, 0.0), axis=1, keepdims=True)
        same = (pn == node) & (piece_ids < here)
        rank = jnp.sum(jnp.where(same, 1.0, 0.0), axis=1, keepdims=True)
        at_mid = mid_node == node
        start = jnp.where(at_mid, root_len, 0.0) + rank * float(seg)
        position = offsets + start
        visible = ((position < sink) | (position >= low)) & (at_mid | (root_node == node))
        r["mask"][:, p * seg : (p + 1) * seg] = jnp.where(visible, 1.0, 0.0)
    my_row = lax.broadcasted_iota(jnp.int32, (nodes, 1), 0) == mine

    def mine_of(values):
        return jnp.sum(jnp.where(my_row, values, 0.0), axis=0, keepdims=True)

    my_finish, my_leaf, my_sink = mine_of(finish), mine_of(leaf_len), mine_of(sink)
    my_low = mine_of(low)
    leaf_offsets = lax.broadcasted_iota(jnp.int32, (8, leaf_max), 1).astype(F32)
    leaf_position = leaf_offsets + (my_finish - my_leaf)
    leaf_visible = ((leaf_position < my_sink) | (leaf_position >= my_low)) & (leaf_offsets < my_leaf)
    r["leaf_mask"][...] = jnp.where(leaf_visible, 1.0, 0.0)

    pq, pkv = r["pq"], r["pkv"]
    pq[:, heads, :] = jnp.zeros((nodes, head_size), F32)
    pkv[:, heads, :] = jnp.zeros((nodes, 2 * head_size), F32)
    loads["w"].wait()
    arrive(0, cols.at[pl.ds(0, nodes - 1)])

    lhs = cols[:, 0, :][:, :width].astype(BF16)
    for h in range(heads):
        pq[:, h, :] = dot(lhs, r["w"][h, :, pl.ds(0, head_size)])
    nq, fq = r["nq"], r["fq"]

    @pl.loop(0, near)
    def _(j):
        tx, tz = neighbour(j)
        src = pq.at[pl.ds((tx * 4 + lax.rem(tz, 4)) * 4, 4)]
        remote(src, nq.at[j], 1, at(tx, tz)).start()

    for h in range(heads):
        pkv[:, h, :] = dot(lhs, r["w"][h, :, pl.ds(head_size, 2 * head_size)])
    arrive(1, nq)
    fq[turn] = pq[owned] + jnp.sum(nq[...], axis=0)
    distant = [lax.rem(z + 4 * d, ZS) for d in (2, 1, 3)]
    for tz in distant:
        remote(fq.at[turn], fq.at[turn], 2, at(x, tz)).start()

    xkv, skv, nkv, tkv, fkv = r["xkv"], r["skv"], r["nkv"], r["tkv"], r["fkv"]
    for dx in range(1, xs):
        tx = across(dx)
        remote(pkv.at[pl.ds(tx * ZS, ZS)], xkv.at[dx - 1], 3, at(tx, z)).start()
    three = pl.ds(0, 3)
    arrive(2, fq.at[three])

    qa = r["qa"]
    qa[owned] = jnp.sum(fq[...], axis=0).astype(BF16)

    @pl.loop(0, near)
    def _(j):
        tx, tz = neighbour(j)
        remote(qa.at[owned], qa.at[owned], 4, at(tx, tz)).start()

    arrive(3, xkv)
    skv[...] = pkv[pl.ds(x * ZS, ZS)] + jnp.sum(xkv[...], axis=0)
    for i, dz in enumerate((2, 1, -1)):
        tz = lax.rem(z + dz + ZS, ZS)
        remote(skv.at[pl.ds(lax.rem(tz, 4) * 4, 4)], nkv.at[i], 5, at(x, tz)).start()

    query = qa[mine]
    row_ids = lax.broadcasted_iota(jnp.int32, (8, 1), 0)
    loads["lk"].wait()
    loads["lv"].wait()
    leaf_scores = jnp.zeros((8, leaf_max), F32)
    for h in range(heads):
        leaf_scores = jnp.where(row_ids == h, dot_t(query, r["lk"][h]), leaf_scores)
    leaf_on = r["leaf_mask"][...] > 0.0
    leaf_scores = jnp.where(leaf_on, leaf_scores * scale, NEGATIVE)
    leaf_m = jnp.max(leaf_scores, axis=1, keepdims=True)
    leaf_w = jnp.where(leaf_on, jnp.exp(leaf_scores - leaf_m), 0.0).astype(BF16)
    leaf_l = jnp.sum(leaf_w.astype(F32), axis=1, keepdims=True)
    leaf_n = jnp.zeros((8, head_size), F32)
    for h in range(heads):
        leaf_n = jnp.where(row_ids == h, dot(leaf_w, r["lv"][h]), leaf_n)

    arrive(5, nkv)
    tkv[...] = skv[pl.ds(lax.rem(z, 4) * 4, 4)] + jnp.sum(nkv[...], axis=0)
    for i, tz in enumerate(distant):
        remote(tkv.at[tz // 4], fkv.at[i], 6, at(x, tz)).start()
    loads["k"].wait()
    loads["v"].wait()
    arrive(4, qa.at[pl.ds(0, near * 4)])

    qf = r["qf"]
    qf[...] = qa[...].astype(F32)
    lanes = lax.broadcasted_iota(jnp.int32, (nodes, 128), 1)
    base = 16 * (lax.broadcasted_iota(jnp.int32, (nodes, 128), 0) % 4)
    stats = jnp.zeros((nodes, 128), F32)
    nb32, nb, st = r["nb32"], r["nb"], r["st"]
    for h in range(heads):
        qh = qf[:, h, :].astype(BF16)
        on = r["mask"][...] > 0.0
        scores = jnp.concatenate([dot_t(qh, r["k"][p, h]) for p in range(seg_dev)], axis=1)
        scores = jnp.where(on, scores * scale, NEGATIVE)
        top = jnp.max(scores, axis=1, keepdims=True)
        weights = jnp.where(on, jnp.exp(scores - top), 0.0).astype(BF16)
        total = jnp.sum(weights.astype(F32), axis=1, keepdims=True)
        summed = dot(weights[:, :seg], r["v"][0, h])
        for p in range(1, seg_dev):
            summed = summed + dot(weights[:, p * seg : (p + 1) * seg], r["v"][p, h])
        nb32[:, h, :] = summed
        stats = jnp.where(lanes == base + h, top, stats)
        stats = jnp.where(lanes == base + (8 + h), total, stats)
    nb32[:, heads, :] = jnp.zeros((nodes, head_size), F32)
    nb[...] = nb32[...].astype(BF16)
    r["st32"][...] = stats
    st[:, 0, :] = sum(r["st32"][pl.ds(i, nodes // 4, stride=4), :] for i in range(4))

    xn, xst, fn, fs = r["xn"], r["xst"], r["fn"], r["fs"]

    @pl.loop(0, near)
    def _(j):
        tx, tz = neighbour(j)
        there = tx * 4 + lax.rem(tz, 4)
        remote(st.at[there], xst.at[j], 7, at(tx, tz)).start()
        remote(nb.at[pl.ds(there * 4, 4)], xn.at[j], 8, at(tx, tz)).start()

    xst[near] = st[block]
    xn[near] = nb[owned]
    upper = lax.broadcasted_iota(jnp.int32, (8, 128), 0)
    lane8 = lax.broadcasted_iota(jnp.int32, (8, 128), 1)
    lane = lax.broadcasted_iota(jnp.int32, (1, 128), 1)
    maximum_lane = lane % 16 < 8

    def upright(row, i):
        spread = jnp.broadcast_to(row, (8, 128))
        return jnp.sum(jnp.where(lane8 == upper + 16 * i, spread, 0.0), axis=1, keepdims=True)

    def flat(col, at_lane):
        spread = jnp.broadcast_to(col, (8, 128))
        return jnp.sum(jnp.where(lane8 == upper + at_lane, spread, 0.0), axis=0, keepdims=True)

    def onward(factors):
        return pltpu.roll(factors, 8, 1)

    arrive(6, fkv)
    new = (tkv[turn] + jnp.sum(fkv[...], axis=0)).astype(BF16).astype(F32)
    own_m = jnp.sum(query.astype(F32) * new[:, :head_size], axis=1, keepdims=True) * scale
    extra_m = jnp.maximum(own_m, leaf_m)
    own_f, leaf_f = jnp.exp(own_m - extra_m), jnp.exp(leaf_m - extra_m)
    extra_l = own_f + leaf_f * leaf_l
    extra_n = own_f * new[:, head_size:] + leaf_f * leaf_n
    my_maxima = (lane >= 16 * turn) & (lane < 16 * turn + 8)
    extra = flat(extra_m, 16 * turn) + flat(extra_l, 16 * turn + 8)
    extra = jnp.where(maximum_lane & ~my_maxima, NEGATIVE, extra)

    arrive(7, xst.at[pl.ds(0, near)])
    stats = xst[:, 0, :]
    top = jnp.maximum(jnp.max(stats, axis=0, keepdims=True), extra)
    factors = jnp.exp(stats - top)
    extra_f = jnp.where(my_maxima, jnp.exp(extra - top), 0.0)
    total = jnp.sum(onward(factors) * stats, axis=0, keepdims=True) + onward(extra_f) * extra
    fs[turn] = jnp.where(maximum_lane, top, total)
    for tz in distant:
        remote(fs.at[turn], fs.at[turn], 9, at(x, tz)).start()
    arrive(8, xn.at[pl.ds(0, near)])
    for i in range(4):
        summed = upright(extra_f, i) * extra_n
        for s in range(near + 1):
            summed = summed + upright(factors[s : s + 1], i) * xn[s, i].astype(F32)
        fn[turn, i] = summed.astype(BF16)
        for tz in distant:
            remote(fn.at[turn, i], fn.at[turn, i], 10, at(x, tz)).start()
    arrive(9, fs.at[three])
    stats = fs[:, 0, :]
    top = jnp.max(stats, axis=0, keepdims=True)
    factors = jnp.exp(stats - top)
    total = jnp.sum(onward(factors) * stats, axis=0, keepdims=True)
    total = pltpu.roll(total, 120, 1)
    factors = factors / jnp.where(maximum_lane & (lane < 64), total, 1.0)
    factors = [[upright(factors[s : s + 1], i) for s in range(4)] for i in range(4)]
    arrive(10, fn.at[three])

    aa = r["aa"]
    for i in range(4):
        attended = sum(factors[i][s] * fn[s, i].astype(F32) for s in range(4))
        aa[block * 4 + i] = attended.astype(BF16)

    @pl.loop(0, near)
    def _(j):
        tx, tz = neighbour(j)
        remote(aa.at[owned], aa.at[owned], 11, at(tx, tz)).start()

    loads["wo"].wait()
    arrive(11, aa.at[pl.ds(0, near * 4)])

    for n in range(nodes):
        qf[n] = aa[rho(n)].astype(F32)
    acc = jnp.zeros((nodes, out_width), F32)
    for h in range(heads):
        acc = acc + dot_t(qf[:, h, :].astype(BF16), r["wo"][:, h * head_size : (h + 1) * head_size])
    rows_out = nodes // heads_n
    os, orr = r["os"], r["orr"]
    os[:, :, pl.ds(0, out_width)] = acc.reshape(heads_n, rows_out, out_width)
    for dh in range(1, heads_n):
        th = lax.rem(hd + dh, heads_n)
        remote(os.at[th], orr.at[dh - 1], 12, {"nodes": me, "heads": th}).start()
    arrive(12, orr)
    result = os[hd] + jnp.sum(orr[...], axis=0)
    r["out"][...] = result[:, :out_width].astype(BF16)

    for sem, ref in sent:
        remote(ref, ref, sem, other).wait_send()


def on_device(
    hidden,
    norm_gain,
    qkv_weight,
    out_weight,
    prefix_keys,
    prefix_values,
    leaf_keys,
    leaf_values,
    piece_node,
    mid_parent,
    leaf_parent,
    leaf_len,
    sink_len,
    window_len,
):
    nodes = lax.axis_size("nodes")
    heads_n = lax.axis_size("heads")
    xs = nodes // ZS
    width, heads, triple = qkv_weight.shape
    head_size = triple // 3
    seg_dev, seg = prefix_keys.shape[:2]
    leaf_max = leaf_keys.shape[1]
    out_width = out_weight.shape[1]
    rows_out = nodes // heads_n
    dims = (nodes, heads_n, heads, head_size, width, seg_dev, seg, leaf_max, out_width)
    large = {
        "hidden_hbm": hidden,
        "gain_hbm": norm_gain[None, :],
        "pn_hbm": piece_node[None, :],
        "mp_hbm": mid_parent[None, :],
        "lp_hbm": leaf_parent[None, :],
        "ll_hbm": leaf_len[None, :],
        "sl_hbm": sink_len[None, :],
        "wl_hbm": window_len[None, :],
        "w_hbm": qkv_weight.transpose(1, 0, 2),
        "wo_hbm": out_weight.T,
        "k_hbm": prefix_keys.transpose(0, 2, 1, 3),
        "v_hbm": prefix_values.transpose(0, 2, 1, 3),
        "lk_hbm": leaf_keys[0].transpose(1, 0, 2),
        "lv_hbm": leaf_values[0].transpose(1, 0, 2),
    }
    vmem = pltpu.VMEM
    scratch = {n[:-4]: vmem(a.shape, a.dtype) for n, a in large.items()}
    scratch |= {
        "rows": vmem((nodes, 1, 128), F32),
        "cols": vmem((nodes, 1, 128), F32),
        "mask": vmem((nodes, seg_dev * seg), F32),
        "leaf_mask": vmem((8, leaf_max), F32),
        "pq": vmem((nodes, 8, head_size), F32),
        "nq": vmem((xs * 4 - 1, 4, 8, head_size), F32),
        "fq": vmem((4, 4, 8, head_size), F32),
        "pkv": vmem((nodes, 8, 2 * head_size), F32),
        "xkv": vmem((xs - 1, ZS, 8, 2 * head_size), F32),
        "skv": vmem((ZS, 8, 2 * head_size), F32),
        "nkv": vmem((3, 4, 8, 2 * head_size), F32),
        "tkv": vmem((4, 8, 2 * head_size), F32),
        "fkv": vmem((3, 8, 2 * head_size), F32),
        "qa": vmem((nodes, 8, head_size), BF16),
        "aa": vmem((nodes, 8, head_size), BF16),
        "qf": vmem((nodes, 8, head_size), F32),
        "nb32": vmem((nodes, 8, head_size), F32),
        "nb": vmem((nodes, 8, head_size), BF16),
        "xn": vmem((xs * 4, 4, 8, head_size), BF16),
        "st32": vmem((nodes, 128), F32),
        "st": vmem((nodes // 4, 1, 128), F32),
        "xst": vmem((xs * 4, 1, 128), F32),
        "fn": vmem((4, 4, 8, head_size), BF16),
        "fs": vmem((4, 1, 128), F32),
        "os": vmem((heads_n, rows_out, 128), F32),
        "orr": vmem((heads_n - 1, rows_out, 128), F32),
        "load": pltpu.SemaphoreType.DMA((len(LOADED),)),
        "send": pltpu.SemaphoreType.DMA((13,)),
        "recv": pltpu.SemaphoreType.DMA((13,)),
    }
    names = list(large) + ["out"] + list(scratch)
    return pl.pallas_call(
        functools.partial(kernel, dims, names),
        out_shape=jax.ShapeDtypeStruct((rows_out, out_width), BF16),
        in_specs=[pl.BlockSpec(memory_space=pl.ANY)] * len(large),
        out_specs=pl.BlockSpec(memory_space=pltpu.VMEM),
        scratch_shapes=list(scratch.values()),
        compiler_params=pltpu.CompilerParams(
            collective_id=0, has_side_effects=True, vmem_limit_bytes=60 * 2**20
        ),
    )(*large.values())


def solution(mesh):
    return jax.shard_map(
        on_device,
        mesh=mesh,
        in_specs=(
            P("nodes", None),
            P(),
            P("nodes", "heads", None),
            P("heads", "nodes"),
            P("nodes", None, "heads", None),
            P("nodes", None, "heads", None),
            P("nodes", None, "heads", None),
            P("nodes", None, "heads", None),
            P(),
            P(),
            P(),
            P(),
            P(),
            P(),
        ),
        out_specs=P("heads", "nodes"),
        check_vma=False,
    )
```

```python
import functools
import math

import jax
import jax.numpy as jnp
from jax import lax
from jax.experimental import pallas as pl
from jax.experimental.pallas import tpu as pltpu
from jax.sharding import PartitionSpec as P

MESH = pl.DeviceIdType.MESH
F32 = jnp.float32
BF16 = jnp.bfloat16
ROOTS = 4
EPSILON = 1e-05
NEGATIVE = -1e30
LOADED = ("hidden", "gain", "pn", "mp", "lp", "ll", "sl", "wl", "w", "k", "v", "lk", "lv", "wo")
SEM = {
    n: i
    for i, n in enumerate(
        ("rows", "twin", "nq0", "nq1", "fq", "qa0", "qa1", "xkv0", "xkv1", "nkv", "fkv", "leaf")
        + ("xst0", "xst1", "xn0", "xn1", "fs", "fn0", "fn1", "aa0", "aa1", "out")
    )
}
ZS = 16


def rho(n):
    z = lax.rem(n, ZS) if not isinstance(n, int) else n % ZS
    return n - z + (z % 4) * 4 + z // 4


def column(row):
    n = row.shape[1]
    i = lax.broadcasted_iota(jnp.int32, (n, n), 0)
    here = (i // ZS) * ZS + (i % 4) * 4 + (i % ZS) // 4 == lax.broadcasted_iota(jnp.int32, (n, n), 1)
    return jnp.sum(jnp.where(here, jnp.broadcast_to(row, (n, n)), 0.0), axis=1, keepdims=True)


def dot_t(a, b):
    return lax.dot_general(a, b, (((1,), (1,)), ((), ())), preferred_element_type=F32)


def dot(a, b):
    return jnp.dot(a, b, preferred_element_type=F32)


def kernel(dims, names, *refs):
    nodes, heads_n, heads, head_size, width, seg_dev, seg, leaf_max, out_width = dims
    r = dict(zip(names, refs, strict=True))
    xs = nodes // ZS
    me = lax.axis_index("nodes")
    hd = lax.axis_index("heads")
    x, z = me // ZS, lax.rem(me, ZS)
    core = lax.rem(hd, 2)
    hub, low, twin = hd + 1 - core, hd - core, hd + 1 - 2 * core
    mine, block, turn = rho(me), x * 4 + lax.rem(z, 4), z // 4
    scale = 1.0 / math.sqrt(head_size)
    near = xs * 4 - 1
    owned = pl.ds(block * 4, 4)
    fifteen, three = pl.ds(0, near), pl.ds(0, 3)

    def at(tx, tz, th):
        return {"nodes": tx * ZS + tz, "heads": th}

    def far(j):
        half = (j + 1) // 2
        return lax.rem(z + ZS // 2 + half * (1 - 2 * lax.rem(j, 2)), ZS)

    def across(j):
        return lax.rem(x + j, xs)

    def offsets_of(j):
        i, k = lax.rem(j, 4), j // 4
        return 2 + ((i + 1) // 2) * (1 - 2 * lax.rem(i, 2)), 2 - k - k // 2 + 2 * (k // 3)

    def neighbour(j):
        dx, dz = offsets_of(j)
        return lax.rem(x + dx, xs), lax.rem(z + dz + ZS, ZS)

    def copy(src, dst, sem, target):
        return pltpu.make_async_remote_copy(
            src_ref=src,
            dst_ref=dst,
            send_sem=r["send"].at[sem],
            recv_sem=r["recv"].at[sem],
            device_id=target,
            device_id_type=MESH,
        )

    def remote(src, dst, sem, target):
        copy(src, dst, SEM[sem] if isinstance(sem, str) else sem, target).start()

    def arrive(sem, ref):
        copy(ref, ref, SEM[sem], at(x, z, twin)).wait_recv()

    def left(sem, ref):
        copy(ref, ref, SEM[sem], at(x, z, twin)).wait_send()

    on_hub, on_low = pl.when(core == 1), pl.when(core == 0)
    distant = [lax.rem(z + 4 * d, ZS) for d in (2, 1, 3)]

    loads = {
        n: pltpu.make_async_copy(r[n + "_hbm"], r[n], r["load"].at[i])
        for i, n in enumerate(LOADED)
    }
    loads["hidden"].start()
    loads["gain"].start()
    barrier = pltpu.get_barrier_semaphore()

    def tell(target):
        pl.semaphore_signal(barrier, inc=1, device_id=target, device_id_type=MESH)

    @on_hub
    def _():
        @pl.loop(0, ZS - 1)
        def _(j):
            for dx in (2, 1, 3, 0):
                tell(at(across(dx), far(j), hd))

        for dx in range(1, xs):
            tell(at(across(dx), z, hd))

    @pl.loop(0, near)
    def _(j):
        dx, dz = offsets_of(j)
        tell(at(lax.rem(x - dx + 2 * xs, xs), lax.rem(z - dz + ZS, ZS), twin))

    for dh in range(1, heads_n):
        tell({"nodes": me, "heads": lax.rem(hd + dh, heads_n)})

    for n in LOADED[2:]:
        loads[n].start()
    loads["hidden"].wait()
    loads["gain"].wait()

    rows, cols = r["rows"], r["cols"]

    @on_hub
    def _():
        values = r["hidden"][...].astype(F32)
        features = values.shape[1]
        mean = jnp.sum(values, axis=1, keepdims=True) * (1.0 / features)
        centered = values - mean
        variance = jnp.sum(centered * centered, axis=1, keepdims=True) * (1.0 / features)
        normed = centered * lax.rsqrt(variance + EPSILON) * r["gain"][...]
        normed = normed.astype(BF16).astype(F32)
        for n in range(nodes):
            rows[n, :, pl.ds(0, width)] = normed[:, n * width : (n + 1) * width]

        pl.semaphore_wait(barrier, nodes - 1 + near + heads_n - 1)

        @pl.loop(0, ZS - 1)
        def _(j):
            tz = far(j)
            for dx in (2, 1, 3, 0):
                tx = across(dx)
                remote(rows.at[tx * ZS + tz], cols.at[mine], "rows", at(tx, tz, hd))

        for dx in range(1, xs):
            tx = across(dx)
            remote(rows.at[tx * ZS + z], cols.at[mine], "rows", at(tx, z, hd))
        cols[mine] = rows[me]

    @on_low
    def _():
        pl.semaphore_wait(barrier, near + heads_n - 1)

    for n in ("pn", "mp", "lp", "ll", "sl", "wl"):
        loads[n].wait()
    pn = r["pn"][...].astype(F32)
    pieces = pn.shape[1]
    mids = r["mp"].shape[1]
    parent = column(r["lp"][...].astype(F32))
    leaf_len = column(r["ll"][...].astype(F32))
    sink = column(r["sl"][...].astype(F32))
    window = column(r["wl"][...].astype(F32))
    mid_ids = lax.broadcasted_iota(jnp.int32, (nodes, mids), 1).astype(F32)
    mp = jnp.broadcast_to(r["mp"][...].astype(F32), (nodes, mids))
    root_node = jnp.sum(jnp.where(mid_ids == parent, mp, 0.0), axis=1, keepdims=True)
    mid_node = parent + float(ROOTS)
    pn_all = jnp.broadcast_to(pn, (nodes, pieces))
    root_len = float(seg) * jnp.sum(jnp.where(pn_all == root_node, 1.0, 0.0), axis=1, keepdims=True)
    mid_len = float(seg) * jnp.sum(jnp.where(pn_all == mid_node, 1.0, 0.0), axis=1, keepdims=True)
    finish = root_len + mid_len + leaf_len
    since = finish - window
    piece_ids = lax.broadcasted_iota(jnp.int32, (1, pieces), 1)
    offsets = lax.broadcasted_iota(jnp.int32, (nodes, seg), 1).astype(F32)
    for p in range(seg_dev):
        here = me * seg_dev + p
        node = jnp.sum(jnp.where(piece_ids == here, pn, 0.0), axis=1, keepdims=True)
        same = (pn == node) & (piece_ids < here)
        rank = jnp.sum(jnp.where(same, 1.0, 0.0), axis=1, keepdims=True)
        at_mid = mid_node == node
        start = jnp.where(at_mid, root_len, 0.0) + rank * float(seg)
        position = offsets + start
        visible = ((position < sink) | (position >= since)) & (at_mid | (root_node == node))
        r["mask"][:, p * seg : (p + 1) * seg] = jnp.where(visible, 1.0, 0.0)
    my_row = lax.broadcasted_iota(jnp.int32, (nodes, 1), 0) == mine

    def mine_of(values):
        return jnp.sum(jnp.where(my_row, values, 0.0), axis=0, keepdims=True)

    my_finish, my_leaf, my_sink = mine_of(finish), mine_of(leaf_len), mine_of(sink)
    my_low = mine_of(since)
    leaf_offsets = lax.broadcasted_iota(jnp.int32, (8, leaf_max), 1).astype(F32)
    leaf_position = leaf_offsets + (my_finish - my_leaf)
    leaf_visible = ((leaf_position < my_sink) | (leaf_position >= my_low)) & (leaf_offsets < my_leaf)
    r["leaf_mask"][...] = jnp.where(leaf_visible, 1.0, 0.0)

    pq, pkv = r["pq"], r["pkv"]
    pq[:, heads, :] = jnp.zeros((nodes, head_size), F32)
    pkv[:, heads, :] = jnp.zeros((nodes, 2 * head_size), F32)
    loads["w"].wait()

    @on_hub
    def _():
        arrive("rows", cols.at[pl.ds(0, nodes - 1)])
        remote(cols, cols, "twin", at(x, z, low))

    @on_low
    def _():
        arrive("twin", cols)

    lhs = cols[:, 0, :][:, :width].astype(BF16)
    for h in range(heads):
        pq[:, h, :] = dot(lhs, r["w"][h, :, pl.ds(0, head_size)])
    nq, fq = r["nq"], r["fq"]

    @pl.loop(0, near)
    def _(j):
        tx, tz = neighbour(j)
        src = pq.at[pl.ds((tx * 4 + lax.rem(tz, 4)) * 4, 4)]
        remote(src, nq.at[core, j], SEM["nq0"] + core, at(tx, tz, hub))

    @on_low
    def _():
        remote(pq.at[owned], nq.at[0, near], "nq0", at(x, z, hub))

    for h in range(heads):
        pkv[:, h, :] = dot(lhs, r["w"][h, :, pl.ds(head_size, 2 * head_size)])

    @on_hub
    def _():
        nq[1, near] = pq[owned]
        arrive("nq1", nq.at[1, fifteen])
        fq[turn, 1] = jnp.sum(nq[1], axis=0)
        arrive("nq0", nq.at[0])
        fq[turn, 0] = jnp.sum(nq[0], axis=0)
        for tz in distant:
            remote(fq.at[turn], fq.at[turn], "fq", at(x, tz, hd))
        pl.semaphore_signal(r["go"], inc=1, device_id=at(x, z, low), device_id_type=MESH)

    @on_low
    def _():
        pl.semaphore_wait(r["go"], 1)

    xkv, skv, nkv, tkv, fkv = r["xkv"], r["skv"], r["nkv"], r["tkv"], r["fkv"]
    row = pl.ds(x * ZS, ZS)
    for dx in range(1, xs):
        tx = across(dx)
        remote(pkv.at[pl.ds(tx * ZS, ZS)], xkv.at[core, dx - 1], SEM["xkv0"] + core, at(tx, z, hub))

    @on_low
    def _():
        remote(pkv.at[row], xkv.at[0, xs - 1], "xkv0", at(x, z, hub))

    qa, q0 = r["qa"], r["q0"]
    row_ids = lax.broadcasted_iota(jnp.int32, (8, 1), 0)
    leaf = r["leaf"]

    def leaf_part(at_core):
        query = qa[mine]
        scores = jnp.zeros((8, leaf_max), F32)
        for h in range(heads):
            scores = jnp.where(row_ids == h, dot_t(query, r["lk"][h]), scores)
        on = r["leaf_mask"][...] > 0.0
        scores = jnp.where(on, scores * scale, NEGATIVE)
        top = jnp.max(scores, axis=1, keepdims=True)
        weights = jnp.where(on, jnp.exp(scores - top), 0.0).astype(BF16)
        summed = jnp.zeros((8, head_size), F32)
        for h in range(heads):
            summed = jnp.where(row_ids == h, dot(weights, r["lv"][h]), summed)
        total = jnp.sum(weights.astype(F32), axis=1, keepdims=True)
        leaf[at_core, 0] = jnp.broadcast_to(top, (8, head_size))
        leaf[at_core, 1] = jnp.broadcast_to(total, (8, head_size))
        leaf[at_core, 2] = summed

    for n in ("lk", "lv", "k", "v"):
        loads[n].wait()

    @on_hub
    def _():
        xkv[1, xs - 1] = pkv[row]
        arrive("fq", fq.at[three])

        q0[...] = (fq[0, 0] + fq[1, 0] + fq[2, 0] + fq[3, 0]).astype(BF16)
        qa[owned] = (fq[0, 1] + fq[1, 1] + fq[2, 1] + fq[3, 1]).astype(BF16)

        @pl.loop(0, near)
        def _(j):
            tx, tz = neighbour(j)
            remote(q0, qa.at[owned], "qa0", at(tx, tz, low))
            remote(qa.at[owned], qa.at[owned], "qa1", at(tx, tz, hd))

        remote(q0, qa.at[owned], "qa0", at(x, z, low))
        arrive("xkv1", xkv.at[1, three])
        arrive("xkv0", xkv.at[0])
        for p in range(2):
            skv[:, p] = jnp.sum(xkv[p], axis=0)
        for i, dz in enumerate((2, 1, -1)):
            tz = lax.rem(z + dz + ZS, ZS)
            remote(skv.at[pl.ds(lax.rem(tz, 4) * 4, 4)], nkv.at[i], "nkv", at(x, tz, hd))
        leaf_part(1)
        arrive("nkv", nkv)
        tkv[...] = skv[pl.ds(lax.rem(z, 4) * 4, 4)] + jnp.sum(nkv[...], axis=0)
        for i, tz in enumerate(distant):
            remote(tkv.at[tz // 4], fkv.at[i], "fkv", at(x, tz, hd))
        arrive("qa1", qa.at[pl.ds(0, near * 4)])

    @on_low
    def _():
        arrive("qa0", qa)

    qf = r["qf"]
    qf[...] = qa[...].astype(F32)
    lanes = lax.broadcasted_iota(jnp.int32, (nodes, 128), 1)
    base = 16 * (lax.broadcasted_iota(jnp.int32, (nodes, 128), 0) % 4)
    stats = jnp.zeros((nodes, 128), F32)
    nb32, nb, st = r["nb32"], r["nb"], r["st"]
    for h in range(heads):
        qh = qf[:, h, :].astype(BF16)
        on = r["mask"][...] > 0.0
        scores = jnp.concatenate([dot_t(qh, r["k"][p, h]) for p in range(seg_dev)], axis=1)
        scores = jnp.where(on, scores * scale, NEGATIVE)
        top = jnp.max(scores, axis=1, keepdims=True)
        weights = jnp.where(on, jnp.exp(scores - top), 0.0).astype(BF16)
        total = jnp.sum(weights.astype(F32), axis=1, keepdims=True)
        summed = dot(weights[:, :seg], r["v"][0, h])
        for p in range(1, seg_dev):
            summed = summed + dot(weights[:, p * seg : (p + 1) * seg], r["v"][p, h])
        nb32[:, h, :] = summed
        stats = jnp.where(lanes == base + h, top, stats)
        stats = jnp.where(lanes == base + (8 + h), total, stats)
    nb32[:, heads, :] = jnp.zeros((nodes, head_size), F32)
    nb[...] = nb32[...].astype(BF16)
    r["st32"][...] = stats
    st[:, 0, :] = sum(r["st32"][pl.ds(i, nodes // 4, stride=4), :] for i in range(4))

    xn, xst, fn, fs = r["xn"], r["xst"], r["fn"], r["fs"]

    @pl.loop(0, near)
    def _(j):
        tx, tz = neighbour(j)
        there = tx * 4 + lax.rem(tz, 4)
        remote(st.at[there], xst.at[core, j], SEM["xst0"] + core, at(tx, tz, hub))
        remote(nb.at[pl.ds(there * 4, 4)], xn.at[core, j], SEM["xn0"] + core, at(tx, tz, hub))

    @on_low
    def _():
        remote(st.at[block], xst.at[0, near], "xst0", at(x, z, hub))
        remote(nb.at[owned], xn.at[0, near], "xn0", at(x, z, hub))
        leaf_part(0)
        remote(leaf.at[0], leaf.at[0], "leaf", at(x, z, hub))

    aa, a0 = r["aa"], r["a0"]
    upper = lax.broadcasted_iota(jnp.int32, (8, 128), 0)
    lane8 = lax.broadcasted_iota(jnp.int32, (8, 128), 1)
    lane = lax.broadcasted_iota(jnp.int32, (1, 128), 1)
    maximum_lane = lane % 16 < 8
    my_maxima = (lane >= 16 * turn) & (lane < 16 * turn + 8)

    def upright(row, i):
        spread = jnp.broadcast_to(row, (8, 128))
        return jnp.sum(jnp.where(lane8 == upper + 16 * i, spread, 0.0), axis=1, keepdims=True)

    def flat(col, at_lane):
        spread = jnp.broadcast_to(col, (8, 128))
        return jnp.sum(jnp.where(lane8 == upper + at_lane, spread, 0.0), axis=0, keepdims=True)

    def onward(factors):
        return pltpu.roll(factors, 8, 1)

    def extra_of(p):
        query = qa[mine] if p else q0[turn]
        new = tkv[turn, p] + fkv[0, p] + fkv[1, p] + fkv[2, p]
        new = new.astype(BF16).astype(F32)
        own_m = jnp.sum(query.astype(F32) * new[:, :head_size], axis=1, keepdims=True) * scale
        leaf_m, leaf_l = leaf[p, 0][:, :1], leaf[p, 1][:, :1]
        top = jnp.maximum(own_m, leaf_m)
        own_f, leaf_f = jnp.exp(own_m - top), jnp.exp(leaf_m - top)
        total = own_f + leaf_f * leaf_l
        extra = flat(top, 16 * turn) + flat(total, 16 * turn + 8)
        extra = jnp.where(maximum_lane & ~my_maxima, NEGATIVE, extra)
        return extra, own_f * new[:, head_size:] + leaf_f * leaf[p, 2]

    @on_hub
    def _():
        xst[1, near] = st[block]
        xn[1, near] = nb[owned]
        arrive("fkv", fkv)
        extras = {1: extra_of(1)}
        factors, extra_f = {}, {}
        for p in (1, 0):
            if p:
                arrive("xst1", xst.at[1, fifteen])
            else:
                arrive("leaf", leaf.at[0])
                extras[0] = extra_of(0)
                arrive("xst0", xst.at[0])
            stats, extra = xst[p, :, 0, :], extras[p][0]
            top = jnp.maximum(jnp.max(stats, axis=0, keepdims=True), extra)
            factors[p] = jnp.exp(stats - top)
            extra_f[p] = jnp.where(my_maxima, jnp.exp(extra - top), 0.0)
            total = jnp.sum(onward(factors[p]) * stats, axis=0, keepdims=True)
            total = total + onward(extra_f[p]) * extra
            fs[turn, p] = jnp.where(maximum_lane, top, total)
        for tz in distant:
            remote(fs.at[turn], fs.at[turn], "fs", at(x, tz, hd))
        for p in (1, 0):
            if p:
                arrive("xn1", xn.at[1, fifteen])
            else:
                arrive("xn0", xn.at[0])
            for i in range(4):
                summed = upright(extra_f[p], i) * extras[p][1]
                for s in range(near + 1):
                    summed = summed + upright(factors[p][s : s + 1], i) * xn[p, s, i].astype(F32)
                fn[turn, p, i] = summed.astype(BF16)
            for tz in distant:
                remote(fn.at[turn, p], fn.at[turn, p], "fn1" if p else "fn0", at(x, tz, hd))
        arrive("fs", fs.at[three])
        for p in (0, 1):
            stats = fs[:, p, 0, :]
            top = jnp.max(stats, axis=0, keepdims=True)
            f = jnp.exp(stats - top)
            total = pltpu.roll(jnp.sum(onward(f) * stats, axis=0, keepdims=True), 120, 1)
            f = f / jnp.where(maximum_lane & (lane < 64), total, 1.0)
            factors[p] = [[upright(f[s : s + 1], i) for s in range(4)] for i in range(4)]
        arrive("fn1", fn.at[three, 1])
        arrive("fn0", fn.at[three, 0])

        for p in (0, 1):
            for i in range(4):
                attended = sum(factors[p][i][s] * fn[s, p, i].astype(F32) for s in range(4))
                if p:
                    aa[block * 4 + i] = attended.astype(BF16)
                else:
                    a0[i] = attended.astype(BF16)

        @pl.loop(0, near)
        def _(j):
            tx, tz = neighbour(j)
            remote(a0, aa.at[owned], "aa0", at(tx, tz, low))
            remote(aa.at[owned], aa.at[owned], "aa1", at(tx, tz, hd))

        remote(a0, aa.at[owned], "aa0", at(x, z, low))

    loads["wo"].wait()

    @on_hub
    def _():
        arrive("aa1", aa.at[pl.ds(0, near * 4)])

    @on_low
    def _():
        arrive("aa0", aa)

    for n in range(nodes):
        qf[n] = aa[rho(n)].astype(F32)
    acc = jnp.zeros((nodes, out_width), F32)
    for h in range(heads):
        acc = acc + dot_t(qf[:, h, :].astype(BF16), r["wo"][:, h * head_size : (h + 1) * head_size])
    rows_out = nodes // heads_n
    os, orr = r["os"], r["orr"]
    os[:, :, pl.ds(0, out_width)] = acc.reshape(heads_n, rows_out, out_width)
    for dh in (4, 3, 5, 2, 6, 1, 7):
        th = lax.rem(hd + dh, heads_n)
        remote(os.at[th], orr.at[dh - 1], "out", {"nodes": me, "heads": th})
    arrive("out", orr)
    result = os[hd] + jnp.sum(orr[...], axis=0)
    r["out"][...] = result[:, :out_width].astype(BF16)

    left("out", orr)

    @on_low
    def _():
        left("nq0", nq.at[0])
        left("xkv0", xkv.at[0])
        left("leaf", leaf.at[0])
        left("xst0", xst.at[0])
        left("xn0", xn.at[0])

    @on_hub
    def _():
        left("rows", cols.at[pl.ds(0, nodes - 1)])
        left("twin", cols)
        left("nq1", nq.at[1, fifteen])
        left("fq", fq.at[three])
        left("qa0", qa)
        left("qa1", qa.at[pl.ds(0, near * 4)])
        left("xkv1", xkv.at[1, three])
        left("nkv", nkv)
        left("fkv", fkv)
        left("xst1", xst.at[1, fifteen])
        left("xn1", xn.at[1, fifteen])
        left("fs", fs.at[three])
        left("fn0", fn.at[three, 0])
        left("fn1", fn.at[three, 1])
        left("aa0", aa)
        left("aa1", aa.at[pl.ds(0, near * 4)])


def on_device(
    hidden,
    norm_gain,
    qkv_weight,
    out_weight,
    prefix_keys,
    prefix_values,
    leaf_keys,
    leaf_values,
    piece_node,
    mid_parent,
    leaf_parent,
    leaf_len,
    sink_len,
    window_len,
):
    nodes = lax.axis_size("nodes")
    heads_n = lax.axis_size("heads")
    xs = nodes // ZS
    width, heads, triple = qkv_weight.shape
    head_size = triple // 3
    seg_dev, seg = prefix_keys.shape[:2]
    leaf_max = leaf_keys.shape[1]
    out_width = out_weight.shape[1]
    rows_out = nodes // heads_n
    dims = (nodes, heads_n, heads, head_size, width, seg_dev, seg, leaf_max, out_width)
    large = {
        "hidden_hbm": hidden,
        "gain_hbm": norm_gain[None, :],
        "pn_hbm": piece_node[None, :],
        "mp_hbm": mid_parent[None, :],
        "lp_hbm": leaf_parent[None, :],
        "ll_hbm": leaf_len[None, :],
        "sl_hbm": sink_len[None, :],
        "wl_hbm": window_len[None, :],
        "w_hbm": qkv_weight.transpose(1, 0, 2),
        "wo_hbm": out_weight.T,
        "k_hbm": prefix_keys.transpose(0, 2, 1, 3),
        "v_hbm": prefix_values.transpose(0, 2, 1, 3),
        "lk_hbm": leaf_keys[0].transpose(1, 0, 2),
        "lv_hbm": leaf_values[0].transpose(1, 0, 2),
    }
    vmem = pltpu.VMEM
    scratch = {n[:-4]: vmem(a.shape, a.dtype) for n, a in large.items()}
    scratch |= {
        "rows": vmem((nodes, 1, 128), F32),
        "cols": vmem((nodes, 1, 128), F32),
        "mask": vmem((nodes, seg_dev * seg), F32),
        "leaf_mask": vmem((8, leaf_max), F32),
        "pq": vmem((nodes, 8, head_size), F32),
        "nq": vmem((2, xs * 4, 4, 8, head_size), F32),
        "fq": vmem((4, 2, 4, 8, head_size), F32),
        "pkv": vmem((nodes, 8, 2 * head_size), F32),
        "xkv": vmem((2, xs, ZS, 8, 2 * head_size), F32),
        "skv": vmem((ZS, 2, 8, 2 * head_size), F32),
        "nkv": vmem((3, 4, 2, 8, 2 * head_size), F32),
        "tkv": vmem((4, 2, 8, 2 * head_size), F32),
        "fkv": vmem((3, 2, 8, 2 * head_size), F32),
        "q0": vmem((4, 8, head_size), BF16),
        "a0": vmem((4, 8, head_size), BF16),
        "leaf": vmem((2, 3, 8, head_size), F32),
        "qa": vmem((nodes, 8, head_size), BF16),
        "aa": vmem((nodes, 8, head_size), BF16),
        "qf": vmem((nodes, 8, head_size), F32),
        "nb32": vmem((nodes, 8, head_size), F32),
        "nb": vmem((nodes, 8, head_size), BF16),
        "xn": vmem((2, xs * 4, 4, 8, head_size), BF16),
        "st32": vmem((nodes, 128), F32),
        "st": vmem((nodes // 4, 1, 128), F32),
        "xst": vmem((2, xs * 4, 1, 128), F32),
        "fn": vmem((4, 2, 4, 8, head_size), BF16),
        "fs": vmem((4, 2, 1, 128), F32),
        "os": vmem((heads_n, rows_out, 128), F32),
        "orr": vmem((heads_n - 1, rows_out, 128), F32),
        "go": pltpu.SemaphoreType.REGULAR,
        "load": pltpu.SemaphoreType.DMA((len(LOADED),)),
        "send": pltpu.SemaphoreType.DMA((len(SEM),)),
        "recv": pltpu.SemaphoreType.DMA((len(SEM),)),
    }
    names = list(large) + ["out"] + list(scratch)
    return pl.pallas_call(
        functools.partial(kernel, dims, names),
        out_shape=jax.ShapeDtypeStruct((rows_out, out_width), BF16),
        in_specs=[pl.BlockSpec(memory_space=pl.ANY)] * len(large),
        out_specs=pl.BlockSpec(memory_space=pltpu.VMEM),
        scratch_shapes=list(scratch.values()),
        compiler_params=pltpu.CompilerParams(
            collective_id=0, has_side_effects=True, vmem_limit_bytes=60 * 2**20
        ),
    )(*large.values())


def solution(mesh):
    return jax.shard_map(
        on_device,
        mesh=mesh,
        in_specs=(
            P("nodes", None),
            P(),
            P("nodes", "heads", None),
            P("heads", "nodes"),
            P("nodes", None, "heads", None),
            P("nodes", None, "heads", None),
            P("nodes", None, "heads", None),
            P("nodes", None, "heads", None),
            P(),
            P(),
            P(),
            P(),
            P(),
            P(),
        ),
        out_specs=P("heads", "nodes"),
        check_vma=False,
    )
```

```python
import functools
import math

import jax
import jax.numpy as jnp
from jax import lax
from jax.experimental import pallas as pl
from jax.experimental.pallas import tpu as pltpu
from jax.sharding import PartitionSpec as P

MESH = pl.DeviceIdType.MESH
F32 = jnp.float32
BF16 = jnp.bfloat16
ROOTS = 4
EPSILON = 1e-05
NEGATIVE = -1e30
LOADED = ("hidden", "gain", "pn", "mp", "lp", "ll", "sl", "wl", "w", "k", "v", "lk", "lv", "wo")
SEM = {
    n: i
    for i, n in enumerate(
        ("rows", "twin", "nq0", "nq1", "fq", "qa0", "qa1", "xkv0", "xkv1", "nkv", "fkv", "leaf")
        + ("xst0", "xst1", "xn0", "xn1", "fs0", "fs1", "fn0", "fn1", "aa0", "aa1", "out")
    )
}
ZS = 16


def rho(n):
    z = lax.rem(n, ZS) if not isinstance(n, int) else n % ZS
    return n - z + (z % 4) * 4 + z // 4


def column(row):
    n = row.shape[1]
    i = lax.broadcasted_iota(jnp.int32, (n, n), 0)
    here = (i // ZS) * ZS + (i % 4) * 4 + (i % ZS) // 4 == lax.broadcasted_iota(jnp.int32, (n, n), 1)
    return jnp.sum(jnp.where(here, jnp.broadcast_to(row, (n, n)), 0.0), axis=1, keepdims=True)


def dot_t(a, b):
    return lax.dot_general(a, b, (((1,), (1,)), ((), ())), preferred_element_type=F32)


def dot(a, b):
    return jnp.dot(a, b, preferred_element_type=F32)


def kernel(dims, names, *refs):
    nodes, heads_n, heads, head_size, width, seg_dev, seg, leaf_max, out_width = dims
    r = dict(zip(names, refs, strict=True))
    xs = nodes // ZS
    me = lax.axis_index("nodes")
    hd = lax.axis_index("heads")
    x, z = me // ZS, lax.rem(me, ZS)
    core = lax.rem(hd, 2)
    hub, low, twin = hd + 1 - core, hd - core, hd + 1 - 2 * core
    mine, block, turn = rho(me), x * 4 + lax.rem(z, 4), z // 4
    scale = 1.0 / math.sqrt(head_size)
    near = xs * 4 - 1
    owned = pl.ds(block * 4, 4)
    fifteen, three = pl.ds(0, near), pl.ds(0, 3)

    def at(tx, tz, th):
        return {"nodes": tx * ZS + tz, "heads": th}

    def far(j):
        half = (j + 1) // 2
        return lax.rem(z + ZS // 2 + half * (1 - 2 * lax.rem(j, 2)), ZS)

    def across(j):
        return lax.rem(x + j, xs)

    def offsets_of(j):
        i, k = lax.rem(j, 4), j // 4
        return 2 + ((i + 1) // 2) * (1 - 2 * lax.rem(i, 2)), 2 - k - k // 2 + 2 * (k // 3)

    def neighbour(j):
        dx, dz = offsets_of(j)
        return lax.rem(x + dx, xs), lax.rem(z + dz + ZS, ZS)

    def copy(src, dst, sem, target):
        return pltpu.make_async_remote_copy(
            src_ref=src,
            dst_ref=dst,
            send_sem=r["send"].at[sem],
            recv_sem=r["recv"].at[sem],
            device_id=target,
            device_id_type=MESH,
        )

    def remote(src, dst, sem, target):
        copy(src, dst, SEM[sem] if isinstance(sem, str) else sem, target).start()

    def arrive(sem, ref):
        copy(ref, ref, SEM[sem], at(x, z, twin)).wait_recv()

    def left(sem, ref):
        copy(ref, ref, SEM[sem], at(x, z, twin)).wait_send()

    on_hub, on_low = pl.when(core == 1), pl.when(core == 0)
    distant = [lax.rem(z + 4 * d, ZS) for d in (2, 1, 3)]

    loads = {
        n: pltpu.make_async_copy(r[n + "_hbm"], r[n], r["load"].at[i])
        for i, n in enumerate(LOADED)
    }
    loads["hidden"].start()
    loads["gain"].start()
    barrier = pltpu.get_barrier_semaphore()

    def tell(target):
        pl.semaphore_signal(barrier, inc=1, device_id=target, device_id_type=MESH)

    @on_hub
    def _():
        @pl.loop(0, ZS - 1)
        def _(j):
            for dx in (2, 1, 3, 0):
                tell(at(across(dx), far(j), hd))

        for dx in range(1, xs):
            tell(at(across(dx), z, hd))

    @pl.loop(0, near)
    def _(j):
        dx, dz = offsets_of(j)
        tell(at(lax.rem(x - dx + 2 * xs, xs), lax.rem(z - dz + ZS, ZS), twin))

    for dh in range(1, heads_n):
        tell({"nodes": me, "heads": lax.rem(hd + dh, heads_n)})

    for n in LOADED[2:]:
        loads[n].start()
    loads["hidden"].wait()
    loads["gain"].wait()

    rows, cols = r["rows"], r["cols"]

    @on_hub
    def _():
        values = r["hidden"][...].astype(F32)
        features = values.shape[1]
        mean = jnp.sum(values, axis=1, keepdims=True) * (1.0 / features)
        centered = values - mean
        variance = jnp.sum(centered * centered, axis=1, keepdims=True) * (1.0 / features)
        normed = centered * lax.rsqrt(variance + EPSILON) * r["gain"][...]
        normed = normed.astype(BF16).astype(F32)
        for n in range(nodes):
            rows[n, :, pl.ds(0, width)] = normed[:, n * width : (n + 1) * width]

        pl.semaphore_wait(barrier, nodes - 1 + near + heads_n - 1)

        @pl.loop(0, ZS - 1)
        def _(j):
            tz = far(j)
            for dx in (2, 1, 3, 0):
                tx = across(dx)
                remote(rows.at[tx * ZS + tz], cols.at[mine], "rows", at(tx, tz, hd))

        for dx in range(1, xs):
            tx = across(dx)
            remote(rows.at[tx * ZS + z], cols.at[mine], "rows", at(tx, z, hd))
        cols[mine] = rows[me]

    @on_low
    def _():
        pl.semaphore_wait(barrier, near + heads_n - 1)

    for n in ("pn", "mp", "lp", "ll", "sl", "wl"):
        loads[n].wait()
    pn = r["pn"][...].astype(F32)
    pieces = pn.shape[1]
    mids = r["mp"].shape[1]
    parent = column(r["lp"][...].astype(F32))
    leaf_len = column(r["ll"][...].astype(F32))
    sink = column(r["sl"][...].astype(F32))
    window = column(r["wl"][...].astype(F32))
    mid_ids = lax.broadcasted_iota(jnp.int32, (nodes, mids), 1).astype(F32)
    mp = jnp.broadcast_to(r["mp"][...].astype(F32), (nodes, mids))
    root_node = jnp.sum(jnp.where(mid_ids == parent, mp, 0.0), axis=1, keepdims=True)
    mid_node = parent + float(ROOTS)
    pn_all = jnp.broadcast_to(pn, (nodes, pieces))
    root_len = float(seg) * jnp.sum(jnp.where(pn_all == root_node, 1.0, 0.0), axis=1, keepdims=True)
    mid_len = float(seg) * jnp.sum(jnp.where(pn_all == mid_node, 1.0, 0.0), axis=1, keepdims=True)
    finish = root_len + mid_len + leaf_len
    since = finish - window
    piece_ids = lax.broadcasted_iota(jnp.int32, (1, pieces), 1)
    offsets = lax.broadcasted_iota(jnp.int32, (nodes, seg), 1).astype(F32)
    for p in range(seg_dev):
        here = me * seg_dev + p
        node = jnp.sum(jnp.where(piece_ids == here, pn, 0.0), axis=1, keepdims=True)
        same = (pn == node) & (piece_ids < here)
        rank = jnp.sum(jnp.where(same, 1.0, 0.0), axis=1, keepdims=True)
        at_mid = mid_node == node
        start = jnp.where(at_mid, root_len, 0.0) + rank * float(seg)
        position = offsets + start
        visible = ((position < sink) | (position >= since)) & (at_mid | (root_node == node))
        r["mask"][:, p * seg : (p + 1) * seg] = jnp.where(visible, 1.0, 0.0)
    my_row = lax.broadcasted_iota(jnp.int32, (nodes, 1), 0) == mine

    def mine_of(values):
        return jnp.sum(jnp.where(my_row, values, 0.0), axis=0, keepdims=True)

    my_finish, my_leaf, my_sink = mine_of(finish), mine_of(leaf_len), mine_of(sink)
    my_low = mine_of(since)
    leaf_offsets = lax.broadcasted_iota(jnp.int32, (8, leaf_max), 1).astype(F32)
    leaf_position = leaf_offsets + (my_finish - my_leaf)
    leaf_visible = ((leaf_position < my_sink) | (leaf_position >= my_low)) & (leaf_offsets < my_leaf)
    r["leaf_mask"][...] = jnp.where(leaf_visible, 1.0, 0.0)

    pq, pkv = r["pq"], r["pkv"]
    pq[:, heads, :] = jnp.zeros((nodes, head_size), F32)
    pkv[:, heads, :] = jnp.zeros((nodes, 2 * head_size), F32)
    loads["w"].wait()

    @on_hub
    def _():
        arrive("rows", cols.at[pl.ds(0, nodes - 1)])
        remote(cols, cols, "twin", at(x, z, low))

    @on_low
    def _():
        arrive("twin", cols)

    lhs = cols[:, 0, :][:, :width].astype(BF16)
    for h in range(heads):
        pq[:, h, :] = dot(lhs, r["w"][h, :, pl.ds(0, head_size)])
    nq, fq = r["nq"], r["fq"]

    @pl.loop(0, near)
    def _(j):
        tx, tz = neighbour(j)
        src = pq.at[pl.ds((tx * 4 + lax.rem(tz, 4)) * 4, 4)]
        remote(src, nq.at[core, j], SEM["nq0"] + core, at(tx, tz, hub))

    @on_low
    def _():
        remote(pq.at[owned], nq.at[0, near], "nq0", at(x, z, hub))

    for h in range(heads):
        pkv[:, h, :] = dot(lhs, r["w"][h, :, pl.ds(head_size, 2 * head_size)])
    pkv16 = r["pkv16"]
    pkv16[...] = pkv[...].astype(BF16)

    xkv, skv, nkv, tkv, fkv = r["xkv"], r["skv"], r["nkv"], r["tkv"], r["fkv"]
    row = pl.ds(x * ZS, ZS)
    for dx in range(1, xs):
        tx = across(dx)
        remote(pkv16.at[pl.ds(tx * ZS, ZS)], xkv.at[core, dx - 1], SEM["xkv0"] + core, at(tx, z, hub))

    @on_low
    def _():
        remote(pkv16.at[row], xkv.at[0, xs - 1], "xkv0", at(x, z, hub))

    @on_hub
    def _():
        nq[1, near] = pq[owned]
        arrive("nq1", nq.at[1, fifteen])
        fq[turn, 1] = jnp.sum(nq[1], axis=0)
        arrive("nq0", nq.at[0])
        fq[turn, 0] = jnp.sum(nq[0], axis=0)
        for tz in distant:
            remote(fq.at[turn], fq.at[turn], "fq", at(x, tz, hd))

    qa, q0 = r["qa"], r["q0"]
    row_ids = lax.broadcasted_iota(jnp.int32, (8, 1), 0)
    leaf = r["leaf"]

    def leaf_part(at_core):
        query = qa[mine]
        scores = jnp.zeros((8, leaf_max), F32)
        for h in range(heads):
            scores = jnp.where(row_ids == h, dot_t(query, r["lk"][h]), scores)
        on = r["leaf_mask"][...] > 0.0
        scores = jnp.where(on, scores * scale, NEGATIVE)
        top = jnp.max(scores, axis=1, keepdims=True)
        weights = jnp.where(on, jnp.exp(scores - top), 0.0).astype(BF16)
        summed = jnp.zeros((8, head_size), F32)
        for h in range(heads):
            summed = jnp.where(row_ids == h, dot(weights, r["lv"][h]), summed)
        total = jnp.sum(weights.astype(F32), axis=1, keepdims=True)
        leaf[at_core, 0] = jnp.broadcast_to(top, (8, head_size))
        leaf[at_core, 1] = jnp.broadcast_to(total, (8, head_size))
        leaf[at_core, 2] = summed

    for n in ("lk", "lv", "k", "v"):
        loads[n].wait()

    @on_hub
    def _():
        xkv[1, xs - 1] = pkv16[row]
        arrive("xkv1", xkv.at[1, three])
        arrive("xkv0", xkv.at[0])
        for p in range(2):
            skv[:, p] = jnp.sum(xkv[p].astype(F32), axis=0)
        for i, dz in enumerate((2, 1, -1)):
            tz = lax.rem(z + dz + ZS, ZS)
            remote(skv.at[pl.ds(lax.rem(tz, 4) * 4, 4)], nkv.at[i], "nkv", at(x, tz, hd))
        arrive("fq", fq.at[three])

        q0[...] = (fq[0, 0] + fq[1, 0] + fq[2, 0] + fq[3, 0]).astype(BF16)
        qa[owned] = (fq[0, 1] + fq[1, 1] + fq[2, 1] + fq[3, 1]).astype(BF16)

        @pl.loop(0, near)
        def _(j):
            tx, tz = neighbour(j)
            remote(q0, qa.at[owned], "qa0", at(tx, tz, low))
            remote(qa.at[owned], qa.at[owned], "qa1", at(tx, tz, hd))

        remote(q0, qa.at[owned], "qa0", at(x, z, low))
        leaf_part(1)
        arrive("nkv", nkv)
        tkv[...] = skv[pl.ds(lax.rem(z, 4) * 4, 4)] + jnp.sum(nkv[...], axis=0)
        for i, tz in enumerate(distant):
            remote(tkv.at[tz // 4], fkv.at[i], "fkv", at(x, tz, hd))
        arrive("qa1", qa.at[pl.ds(0, near * 4)])

    @on_low
    def _():
        arrive("qa0", qa)

    qf = r["qf"]
    qf[...] = qa[...].astype(F32)
    lanes = lax.broadcasted_iota(jnp.int32, (nodes, 128), 1)
    base = 16 * (lax.broadcasted_iota(jnp.int32, (nodes, 128), 0) % 4)
    stats = jnp.zeros((nodes, 128), F32)
    nb32, nb, st = r["nb32"], r["nb"], r["st"]
    for h in range(heads):
        qh = qf[:, h, :].astype(BF16)
        on = r["mask"][...] > 0.0
        scores = jnp.concatenate([dot_t(qh, r["k"][p, h]) for p in range(seg_dev)], axis=1)
        scores = jnp.where(on, scores * scale, NEGATIVE)
        top = jnp.max(scores, axis=1, keepdims=True)
        weights = jnp.where(on, jnp.exp(scores - top), 0.0).astype(BF16)
        total = jnp.sum(weights.astype(F32), axis=1, keepdims=True)
        summed = dot(weights[:, :seg], r["v"][0, h])
        for p in range(1, seg_dev):
            summed = summed + dot(weights[:, p * seg : (p + 1) * seg], r["v"][p, h])
        nb32[:, h, :] = summed
        stats = jnp.where(lanes == base + h, top, stats)
        stats = jnp.where(lanes == base + (8 + h), total, stats)
    nb32[:, heads, :] = jnp.zeros((nodes, head_size), F32)
    nb[...] = nb32[...].astype(BF16)
    r["st32"][...] = stats
    st[:, 0, :] = sum(r["st32"][pl.ds(i, nodes // 4, stride=4), :] for i in range(4))

    xn, xst, fn, fs = r["xn"], r["xst"], r["fn"], r["fs"]

    @pl.loop(0, near)
    def _(j):
        tx, tz = neighbour(j)
        there = tx * 4 + lax.rem(tz, 4)
        remote(st.at[there], xst.at[core, j], SEM["xst0"] + core, at(tx, tz, hub))
        remote(nb.at[pl.ds(there * 4, 4)], xn.at[core, j], SEM["xn0"] + core, at(tx, tz, hub))

    @on_low
    def _():
        remote(st.at[block], xst.at[0, near], "xst0", at(x, z, hub))
        remote(nb.at[owned], xn.at[0, near], "xn0", at(x, z, hub))
        leaf_part(0)
        remote(leaf.at[0], leaf.at[0], "leaf", at(x, z, hub))

    aa, a0 = r["aa"], r["a0"]
    upper = lax.broadcasted_iota(jnp.int32, (8, 128), 0)
    lane8 = lax.broadcasted_iota(jnp.int32, (8, 128), 1)
    lane = lax.broadcasted_iota(jnp.int32, (1, 128), 1)
    maximum_lane = lane % 16 < 8
    my_maxima = (lane >= 16 * turn) & (lane < 16 * turn + 8)

    def upright(row, i):
        spread = jnp.broadcast_to(row, (8, 128))
        return jnp.sum(jnp.where(lane8 == upper + 16 * i, spread, 0.0), axis=1, keepdims=True)

    def flat(col, at_lane):
        spread = jnp.broadcast_to(col, (8, 128))
        return jnp.sum(jnp.where(lane8 == upper + at_lane, spread, 0.0), axis=0, keepdims=True)

    def onward(factors):
        return pltpu.roll(factors, 8, 1)

    def extra_of(p):
        query = qa[mine] if p else q0[turn]
        new = tkv[turn, p] + fkv[0, p] + fkv[1, p] + fkv[2, p]
        new = new.astype(BF16).astype(F32)
        own_m = jnp.sum(query.astype(F32) * new[:, :head_size], axis=1, keepdims=True) * scale
        leaf_m, leaf_l = leaf[p, 0][:, :1], leaf[p, 1][:, :1]
        top = jnp.maximum(own_m, leaf_m)
        own_f, leaf_f = jnp.exp(own_m - top), jnp.exp(leaf_m - top)
        total = own_f + leaf_f * leaf_l
        extra = flat(top, 16 * turn) + flat(total, 16 * turn + 8)
        extra = jnp.where(maximum_lane & ~my_maxima, NEGATIVE, extra)
        return extra, own_f * new[:, head_size:] + leaf_f * leaf[p, 2]

    @on_hub
    def _():
        xst[1, near] = st[block]
        xn[1, near] = nb[owned]
        arrive("fkv", fkv)
        extras = extra_of(1)
        for p in (1, 0):
            arrive("xst1" if p else "xst0", xst.at[1, fifteen] if p else xst.at[0])
            stats, (extra, extra_n) = xst[p, :, 0, :], extras
            top = jnp.maximum(jnp.max(stats, axis=0, keepdims=True), extra)
            factors = jnp.exp(stats - top)
            extra_f = jnp.where(my_maxima, jnp.exp(extra - top), 0.0)
            total = jnp.sum(onward(factors) * stats, axis=0, keepdims=True)
            total = total + onward(extra_f) * extra
            fs[turn, p] = jnp.where(maximum_lane, top, total)
            for tz in distant:
                remote(fs.at[turn, p], fs.at[turn, p], "fs1" if p else "fs0", at(x, tz, hd))
            arrive("xn1" if p else "xn0", xn.at[1, fifteen] if p else xn.at[0])
            for i in range(4):
                summed = upright(extra_f, i) * extra_n
                for s in range(near + 1):
                    summed = summed + upright(factors[s : s + 1], i) * xn[p, s, i].astype(F32)
                fn[turn, p, i] = summed.astype(BF16)
            for tz in distant:
                remote(fn.at[turn, p], fn.at[turn, p], "fn1" if p else "fn0", at(x, tz, hd))
            if p:
                arrive("leaf", leaf.at[0])
                extras = extra_of(0)

        for p in (1, 0):
            arrive("fs1" if p else "fs0", fs.at[three, p])
            stats = fs[:, p, 0, :]
            top = jnp.max(stats, axis=0, keepdims=True)
            f = jnp.exp(stats - top)
            total = pltpu.roll(jnp.sum(onward(f) * stats, axis=0, keepdims=True), 120, 1)
            f = f / jnp.where(maximum_lane & (lane < 64), total, 1.0)
            f = [[upright(f[s : s + 1], i) for s in range(4)] for i in range(4)]
            arrive("fn1" if p else "fn0", fn.at[three, p])
            for i in range(4):
                attended = sum(f[i][s] * fn[s, p, i].astype(F32) for s in range(4))
                if p:
                    aa[block * 4 + i] = attended.astype(BF16)
                else:
                    a0[i] = attended.astype(BF16)
            if p:

                @pl.loop(0, near)
                def _(j):
                    tx, tz = neighbour(j)
                    remote(aa.at[owned], aa.at[owned], "aa1", at(tx, tz, hd))

        @pl.loop(0, near)
        def _(j):
            tx, tz = neighbour(j)
            remote(a0, aa.at[owned], "aa0", at(tx, tz, low))

        remote(a0, aa.at[owned], "aa0", at(x, z, low))

    loads["wo"].wait()

    @on_hub
    def _():
        arrive("aa1", aa.at[pl.ds(0, near * 4)])

    @on_low
    def _():
        arrive("aa0", aa)

    for n in range(nodes):
        qf[n] = aa[rho(n)].astype(F32)
    acc = jnp.zeros((nodes, out_width), F32)
    for h in range(heads):
        acc = acc + dot_t(qf[:, h, :].astype(BF16), r["wo"][:, h * head_size : (h + 1) * head_size])
    rows_out = nodes // heads_n
    os, orr = r["os"], r["orr"]
    os[:, :, pl.ds(0, out_width)] = acc.reshape(heads_n, rows_out, out_width)
    for dh in (4, 3, 5, 2, 6, 1, 7):
        th = lax.rem(hd + dh, heads_n)
        remote(os.at[th], orr.at[dh - 1], "out", {"nodes": me, "heads": th})
    arrive("out", orr)
    result = os[hd] + jnp.sum(orr[...], axis=0)
    r["out"][...] = result[:, :out_width].astype(BF16)

    left("out", orr)

    @on_low
    def _():
        left("nq0", nq.at[0])
        left("xkv0", xkv.at[0])
        left("leaf", leaf.at[0])
        left("xst0", xst.at[0])
        left("xn0", xn.at[0])

    @on_hub
    def _():
        left("rows", cols.at[pl.ds(0, nodes - 1)])
        left("twin", cols)
        left("nq1", nq.at[1, fifteen])
        left("fq", fq.at[three])
        left("qa0", qa)
        left("qa1", qa.at[pl.ds(0, near * 4)])
        left("xkv1", xkv.at[1, three])
        left("nkv", nkv)
        left("fkv", fkv)
        left("xst1", xst.at[1, fifteen])
        left("xn1", xn.at[1, fifteen])
        left("fs0", fs.at[three, 0])
        left("fs1", fs.at[three, 1])
        left("fn0", fn.at[three, 0])
        left("fn1", fn.at[three, 1])
        left("aa0", aa)
        left("aa1", aa.at[pl.ds(0, near * 4)])


def on_device(
    hidden,
    norm_gain,
    qkv_weight,
    out_weight,
    prefix_keys,
    prefix_values,
    leaf_keys,
    leaf_values,
    piece_node,
    mid_parent,
    leaf_parent,
    leaf_len,
    sink_len,
    window_len,
):
    nodes = lax.axis_size("nodes")
    heads_n = lax.axis_size("heads")
    xs = nodes // ZS
    width, heads, triple = qkv_weight.shape
    head_size = triple // 3
    seg_dev, seg = prefix_keys.shape[:2]
    leaf_max = leaf_keys.shape[1]
    out_width = out_weight.shape[1]
    rows_out = nodes // heads_n
    dims = (nodes, heads_n, heads, head_size, width, seg_dev, seg, leaf_max, out_width)
    large = {
        "hidden_hbm": hidden,
        "gain_hbm": norm_gain[None, :],
        "pn_hbm": piece_node[None, :],
        "mp_hbm": mid_parent[None, :],
        "lp_hbm": leaf_parent[None, :],
        "ll_hbm": leaf_len[None, :],
        "sl_hbm": sink_len[None, :],
        "wl_hbm": window_len[None, :],
        "w_hbm": qkv_weight.transpose(1, 0, 2),
        "wo_hbm": out_weight.T,
        "k_hbm": prefix_keys.transpose(0, 2, 1, 3),
        "v_hbm": prefix_values.transpose(0, 2, 1, 3),
        "lk_hbm": leaf_keys[0].transpose(1, 0, 2),
        "lv_hbm": leaf_values[0].transpose(1, 0, 2),
    }
    vmem = pltpu.VMEM
    scratch = {n[:-4]: vmem(a.shape, a.dtype) for n, a in large.items()}
    scratch |= {
        "rows": vmem((nodes, 1, 128), F32),
        "cols": vmem((nodes, 1, 128), F32),
        "mask": vmem((nodes, seg_dev * seg), F32),
        "leaf_mask": vmem((8, leaf_max), F32),
        "pq": vmem((nodes, 8, head_size), F32),
        "nq": vmem((2, xs * 4, 4, 8, head_size), F32),
        "fq": vmem((4, 2, 4, 8, head_size), F32),
        "pkv": vmem((nodes, 8, 2 * head_size), F32),
        "pkv16": vmem((nodes, 8, 2 * head_size), BF16),
        "xkv": vmem((2, xs, ZS, 8, 2 * head_size), BF16),
        "skv": vmem((ZS, 2, 8, 2 * head_size), F32),
        "nkv": vmem((3, 4, 2, 8, 2 * head_size), F32),
        "tkv": vmem((4, 2, 8, 2 * head_size), F32),
        "fkv": vmem((3, 2, 8, 2 * head_size), F32),
        "q0": vmem((4, 8, head_size), BF16),
        "a0": vmem((4, 8, head_size), BF16),
        "leaf": vmem((2, 3, 8, head_size), F32),
        "qa": vmem((nodes, 8, head_size), BF16),
        "aa": vmem((nodes, 8, head_size), BF16),
        "qf": vmem((nodes, 8, head_size), F32),
        "nb32": vmem((nodes, 8, head_size), F32),
        "nb": vmem((nodes, 8, head_size), BF16),
        "xn": vmem((2, xs * 4, 4, 8, head_size), BF16),
        "st32": vmem((nodes, 128), F32),
        "st": vmem((nodes // 4, 1, 128), F32),
        "xst": vmem((2, xs * 4, 1, 128), F32),
        "fn": vmem((4, 2, 4, 8, head_size), BF16),
        "fs": vmem((4, 2, 1, 128), F32),
        "os": vmem((heads_n, rows_out, 128), F32),
        "orr": vmem((heads_n - 1, rows_out, 128), F32),
        "load": pltpu.SemaphoreType.DMA((len(LOADED),)),
        "send": pltpu.SemaphoreType.DMA((len(SEM),)),
        "recv": pltpu.SemaphoreType.DMA((len(SEM),)),
    }
    names = list(large) + ["out"] + list(scratch)
    return pl.pallas_call(
        functools.partial(kernel, dims, names),
        out_shape=jax.ShapeDtypeStruct((rows_out, out_width), BF16),
        in_specs=[pl.BlockSpec(memory_space=pl.ANY)] * len(large),
        out_specs=pl.BlockSpec(memory_space=pltpu.VMEM),
        scratch_shapes=list(scratch.values()),
        compiler_params=pltpu.CompilerParams(
            collective_id=0, has_side_effects=True, vmem_limit_bytes=60 * 2**20
        ),
    )(*large.values())


def solution(mesh):
    return jax.shard_map(
        on_device,
        mesh=mesh,
        in_specs=(
            P("nodes", None),
            P(),
            P("nodes", "heads", None),
            P("heads", "nodes"),
            P("nodes", None, "heads", None),
            P("nodes", None, "heads", None),
            P("nodes", None, "heads", None),
            P("nodes", None, "heads", None),
            P(),
            P(),
            P(),
            P(),
            P(),
            P(),
        ),
        out_specs=P("heads", "nodes"),
        check_vma=False,
    )
```

```python
import functools
import math

import jax
import jax.numpy as jnp
from jax import lax
from jax.experimental import pallas as pl
from jax.experimental.pallas import tpu as pltpu
from jax.sharding import PartitionSpec as P

MESH = pl.DeviceIdType.MESH
F32 = jnp.float32
BF16 = jnp.bfloat16
ROOTS = 4
EPSILON = 1e-05
NEGATIVE = -1e30
LOADED = ("hidden", "gain", "pn", "mp", "lp", "ll", "sl", "wl", "w", "k", "v", "lk", "lv", "wo")
SEM = {
    n: i
    for i, n in enumerate(
        ("rows", "twin", "nq0", "nq1", "fq0", "fq1", "qa0", "qa1", "xkv0", "xkv1", "nkv", "fkv", "leaf")
        + ("xst0", "xst1", "xn0", "xn1", "fs0", "fs1", "fn0", "fn1", "aa0", "aa1", "out")
    )
}
ZS = 16


def rho(n):
    z = lax.rem(n, ZS) if not isinstance(n, int) else n % ZS
    return n - z + (z % 4) * 4 + z // 4


def column(row):
    n = row.shape[1]
    i = lax.broadcasted_iota(jnp.int32, (n, n), 0)
    here = (i // ZS) * ZS + (i % 4) * 4 + (i % ZS) // 4 == lax.broadcasted_iota(jnp.int32, (n, n), 1)
    return jnp.sum(jnp.where(here, jnp.broadcast_to(row, (n, n)), 0.0), axis=1, keepdims=True)


def dot_t(a, b):
    return lax.dot_general(a, b, (((1,), (1,)), ((), ())), preferred_element_type=F32)


def dot(a, b):
    return jnp.dot(a, b, preferred_element_type=F32)


def kernel(dims, names, *refs):
    nodes, heads_n, heads, head_size, width, seg_dev, seg, leaf_max, out_width = dims
    r = dict(zip(names, refs, strict=True))
    xs = nodes // ZS
    me = lax.axis_index("nodes")
    hd = lax.axis_index("heads")
    x, z = me // ZS, lax.rem(me, ZS)
    core = lax.rem(hd, 2)
    hub, low, twin = hd + 1 - core, hd - core, hd + 1 - 2 * core
    mine, block, turn = rho(me), x * 4 + lax.rem(z, 4), z // 4
    scale = 1.0 / math.sqrt(head_size)
    near = xs * 4 - 1
    owned = pl.ds(block * 4, 4)
    fifteen, three = pl.ds(0, near), pl.ds(0, 3)

    def at(tx, tz, th):
        return {"nodes": tx * ZS + tz, "heads": th}

    def far(j):
        half = (j + 1) // 2
        return lax.rem(z + ZS // 2 + half * (1 - 2 * lax.rem(j, 2)), ZS)

    def across(j):
        return lax.rem(x + j, xs)

    def offsets_of(j):
        i, k = lax.rem(j, 4), j // 4
        return 2 + ((i + 1) // 2) * (1 - 2 * lax.rem(i, 2)), 2 - k - k // 2 + 2 * (k // 3)

    def neighbour(j):
        dx, dz = offsets_of(j)
        return lax.rem(x + dx, xs), lax.rem(z + dz + ZS, ZS)

    def copy(src, dst, sem, target):
        return pltpu.make_async_remote_copy(
            src_ref=src,
            dst_ref=dst,
            send_sem=r["send"].at[sem],
            recv_sem=r["recv"].at[sem],
            device_id=target,
            device_id_type=MESH,
        )

    def remote(src, dst, sem, target):
        copy(src, dst, SEM[sem] if isinstance(sem, str) else sem, target).start()

    def arrive(sem, ref):
        copy(ref, ref, SEM[sem], at(x, z, twin)).wait_recv()

    def left(sem, ref):
        copy(ref, ref, SEM[sem], at(x, z, twin)).wait_send()

    on_hub, on_low = pl.when(core == 1), pl.when(core == 0)
    distant = [lax.rem(z + 4 * d, ZS) for d in (2, 1, 3)]

    loads = {
        n: pltpu.make_async_copy(r[n + "_hbm"], r[n], r["load"].at[i])
        for i, n in enumerate(LOADED)
    }
    loads["hidden"].start()
    loads["gain"].start()
    barrier = pltpu.get_barrier_semaphore()

    def tell(target):
        pl.semaphore_signal(barrier, inc=1, device_id=target, device_id_type=MESH)

    @on_hub
    def _():
        @pl.loop(0, ZS - 1)
        def _(j):
            for dx in (2, 1, 3, 0):
                tell(at(across(dx), far(j), hd))

        for dx in range(1, xs):
            tell(at(across(dx), z, hd))

    @pl.loop(0, near)
    def _(j):
        dx, dz = offsets_of(j)
        tell(at(lax.rem(x - dx + 2 * xs, xs), lax.rem(z - dz + ZS, ZS), twin))

    for dh in range(1, heads_n):
        tell({"nodes": me, "heads": lax.rem(hd + dh, heads_n)})

    for n in LOADED[2:]:
        loads[n].start()
    loads["hidden"].wait()
    loads["gain"].wait()

    rows, cols = r["rows"], r["cols"]

    @on_hub
    def _():
        values = r["hidden"][...].astype(F32)
        features = values.shape[1]
        mean = jnp.sum(values, axis=1, keepdims=True) * (1.0 / features)
        centered = values - mean
        variance = jnp.sum(centered * centered, axis=1, keepdims=True) * (1.0 / features)
        normed = centered * lax.rsqrt(variance + EPSILON) * r["gain"][...]
        normed = normed.astype(BF16).astype(F32)
        for n in range(nodes):
            rows[n, :, pl.ds(0, width)] = normed[:, n * width : (n + 1) * width]

        pl.semaphore_wait(barrier, nodes - 1 + near + heads_n - 1)

        @pl.loop(0, ZS - 1)
        def _(j):
            tz = far(j)
            for dx in (2, 1, 3, 0):
                tx = across(dx)
                remote(rows.at[tx * ZS + tz], cols.at[mine], "rows", at(tx, tz, hd))

        for dx in range(1, xs):
            tx = across(dx)
            remote(rows.at[tx * ZS + z], cols.at[mine], "rows", at(tx, z, hd))
        cols[mine] = rows[me]

    @on_low
    def _():
        pl.semaphore_wait(barrier, near + heads_n - 1)

    for n in ("pn", "mp", "lp", "ll", "sl", "wl"):
        loads[n].wait()
    pn = r["pn"][...].astype(F32)
    pieces = pn.shape[1]
    mids = r["mp"].shape[1]
    parent = column(r["lp"][...].astype(F32))
    leaf_len = column(r["ll"][...].astype(F32))
    sink = column(r["sl"][...].astype(F32))
    window = column(r["wl"][...].astype(F32))
    mid_ids = lax.broadcasted_iota(jnp.int32, (nodes, mids), 1).astype(F32)
    mp = jnp.broadcast_to(r["mp"][...].astype(F32), (nodes, mids))
    root_node = jnp.sum(jnp.where(mid_ids == parent, mp, 0.0), axis=1, keepdims=True)
    mid_node = parent + float(ROOTS)
    pn_all = jnp.broadcast_to(pn, (nodes, pieces))
    root_len = float(seg) * jnp.sum(jnp.where(pn_all == root_node, 1.0, 0.0), axis=1, keepdims=True)
    mid_len = float(seg) * jnp.sum(jnp.where(pn_all == mid_node, 1.0, 0.0), axis=1, keepdims=True)
    finish = root_len + mid_len + leaf_len
    since = finish - window
    piece_ids = lax.broadcasted_iota(jnp.int32, (1, pieces), 1)
    offsets = lax.broadcasted_iota(jnp.int32, (nodes, seg), 1).astype(F32)
    for p in range(seg_dev):
        here = me * seg_dev + p
        node = jnp.sum(jnp.where(piece_ids == here, pn, 0.0), axis=1, keepdims=True)
        same = (pn == node) & (piece_ids < here)
        rank = jnp.sum(jnp.where(same, 1.0, 0.0), axis=1, keepdims=True)
        at_mid = mid_node == node
        start = jnp.where(at_mid, root_len, 0.0) + rank * float(seg)
        position = offsets + start
        visible = ((position < sink) | (position >= since)) & (at_mid | (root_node == node))
        r["mask"][:, p * seg : (p + 1) * seg] = jnp.where(visible, 1.0, 0.0)
    my_row = lax.broadcasted_iota(jnp.int32, (nodes, 1), 0) == mine

    def mine_of(values):
        return jnp.sum(jnp.where(my_row, values, 0.0), axis=0, keepdims=True)

    my_finish, my_leaf, my_sink = mine_of(finish), mine_of(leaf_len), mine_of(sink)
    my_low = mine_of(since)
    leaf_offsets = lax.broadcasted_iota(jnp.int32, (8, leaf_max), 1).astype(F32)
    leaf_position = leaf_offsets + (my_finish - my_leaf)
    leaf_visible = ((leaf_position < my_sink) | (leaf_position >= my_low)) & (leaf_offsets < my_leaf)
    r["leaf_mask"][...] = jnp.where(leaf_visible, 1.0, 0.0)

    pq, pkv = r["pq"], r["pkv"]
    pq[:, heads, :] = jnp.zeros((nodes, head_size), F32)
    pkv[:, heads, :] = jnp.zeros((nodes, 2 * head_size), F32)
    loads["w"].wait()

    @on_hub
    def _():
        arrive("rows", cols.at[pl.ds(0, nodes - 1)])
        remote(cols, cols, "twin", at(x, z, low))

    @on_low
    def _():
        arrive("twin", cols)

    lhs = cols[:, 0, :][:, :width].astype(BF16)
    for h in range(heads):
        pq[:, h, :] = dot(lhs, r["w"][h, :, pl.ds(0, head_size)])
    nq, fq = r["nq"], r["fq"]

    @pl.loop(0, near)
    def _(j):
        tx, tz = neighbour(j)
        src = pq.at[pl.ds((tx * 4 + lax.rem(tz, 4)) * 4, 4)]
        remote(src, nq.at[core, j], SEM["nq0"] + core, at(tx, tz, hub))

    @on_low
    def _():
        remote(pq.at[owned], nq.at[0, near], "nq0", at(x, z, hub))

    for h in range(heads):
        pkv[:, h, :] = dot(lhs, r["w"][h, :, pl.ds(head_size, 2 * head_size)])
    pkv16 = r["pkv16"]
    pkv16[...] = pkv[...].astype(BF16)

    xkv, skv, nkv, tkv, fkv = r["xkv"], r["skv"], r["nkv"], r["tkv"], r["fkv"]
    row = pl.ds(x * ZS, ZS)
    for dx in range(1, xs):
        tx = across(dx)
        remote(pkv16.at[pl.ds(tx * ZS, ZS)], xkv.at[core, dx - 1], SEM["xkv0"] + core, at(tx, z, hub))

    @on_low
    def _():
        remote(pkv16.at[row], xkv.at[0, xs - 1], "xkv0", at(x, z, hub))

    @on_hub
    def _():
        nq[1, near] = pq[owned]
        arrive("nq1", nq.at[1, fifteen])
        fq[turn, 1] = jnp.sum(nq[1], axis=0)
        for tz in distant:
            remote(fq.at[turn, 1], fq.at[turn, 1], "fq1", at(x, tz, hd))
        arrive("nq0", nq.at[0])
        fq[turn, 0] = jnp.sum(nq[0], axis=0)
        for tz in distant:
            remote(fq.at[turn, 0], fq.at[turn, 0], "fq0", at(x, tz, hd))

    qa, q0 = r["qa"], r["q0"]
    row_ids = lax.broadcasted_iota(jnp.int32, (8, 1), 0)
    leaf = r["leaf"]

    def leaf_part(at_core):
        query = qa[mine]
        scores = jnp.zeros((8, leaf_max), F32)
        for h in range(heads):
            scores = jnp.where(row_ids == h, dot_t(query, r["lk"][h]), scores)
        on = r["leaf_mask"][...] > 0.0
        scores = jnp.where(on, scores * scale, NEGATIVE)
        top = jnp.max(scores, axis=1, keepdims=True)
        weights = jnp.where(on, jnp.exp(scores - top), 0.0).astype(BF16)
        summed = jnp.zeros((8, head_size), F32)
        for h in range(heads):
            summed = jnp.where(row_ids == h, dot(weights, r["lv"][h]), summed)
        total = jnp.sum(weights.astype(F32), axis=1, keepdims=True)
        leaf[at_core, 0] = jnp.broadcast_to(top, (8, head_size))
        leaf[at_core, 1] = jnp.broadcast_to(total, (8, head_size))
        leaf[at_core, 2] = summed

    for n in ("lk", "lv", "k", "v"):
        loads[n].wait()

    @on_hub
    def _():
        xkv[1, xs - 1] = pkv16[row]
        arrive("xkv1", xkv.at[1, three])
        arrive("xkv0", xkv.at[0])
        for p in range(2):
            skv[:, p] = jnp.sum(xkv[p].astype(F32), axis=0)
        for i, dz in enumerate((2, 1, -1)):
            tz = lax.rem(z + dz + ZS, ZS)
            remote(skv.at[pl.ds(lax.rem(tz, 4) * 4, 4)], nkv.at[i], "nkv", at(x, tz, hd))
        arrive("fq1", fq.at[three, 1])

        qa[owned] = (fq[0, 1] + fq[1, 1] + fq[2, 1] + fq[3, 1]).astype(BF16)

        @pl.loop(0, near)
        def _(j):
            tx, tz = neighbour(j)
            remote(qa.at[owned], qa.at[owned], "qa1", at(tx, tz, hd))

        arrive("fq0", fq.at[three, 0])
        q0[...] = (fq[0, 0] + fq[1, 0] + fq[2, 0] + fq[3, 0]).astype(BF16)

        @pl.loop(0, near)
        def _(j):
            tx, tz = neighbour(j)
            remote(q0, qa.at[owned], "qa0", at(tx, tz, low))

        remote(q0, qa.at[owned], "qa0", at(x, z, low))
        leaf_part(1)
        arrive("nkv", nkv)
        tkv[...] = skv[pl.ds(lax.rem(z, 4) * 4, 4)] + jnp.sum(nkv[...], axis=0)
        for i, tz in enumerate(distant):
            remote(tkv.at[tz // 4], fkv.at[i], "fkv", at(x, tz, hd))
        arrive("qa1", qa.at[pl.ds(0, near * 4)])

    @on_low
    def _():
        arrive("qa0", qa)

    qf = r["qf"]
    qf[...] = qa[...].astype(F32)
    lanes = lax.broadcasted_iota(jnp.int32, (nodes, 128), 1)
    base = 16 * (lax.broadcasted_iota(jnp.int32, (nodes, 128), 0) % 4)
    stats = jnp.zeros((nodes, 128), F32)
    nb32, nb, st = r["nb32"], r["nb"], r["st"]
    for h in range(heads):
        qh = qf[:, h, :].astype(BF16)
        on = r["mask"][...] > 0.0
        scores = jnp.concatenate([dot_t(qh, r["k"][p, h]) for p in range(seg_dev)], axis=1)
        scores = jnp.where(on, scores * scale, NEGATIVE)
        top = jnp.max(scores, axis=1, keepdims=True)
        weights = jnp.where(on, jnp.exp(scores - top), 0.0).astype(BF16)
        total = jnp.sum(weights.astype(F32), axis=1, keepdims=True)
        summed = dot(weights[:, :seg], r["v"][0, h])
        for p in range(1, seg_dev):
            summed = summed + dot(weights[:, p * seg : (p + 1) * seg], r["v"][p, h])
        nb32[:, h, :] = summed
        stats = jnp.where(lanes == base + h, top, stats)
        stats = jnp.where(lanes == base + (8 + h), total, stats)
    nb32[:, heads, :] = jnp.zeros((nodes, head_size), F32)
    nb[...] = nb32[...].astype(BF16)
    r["st32"][...] = stats
    st[:, 0, :] = sum(r["st32"][pl.ds(i, nodes // 4, stride=4), :] for i in range(4))

    xn, xst, fn, fs = r["xn"], r["xst"], r["fn"], r["fs"]

    @pl.loop(0, near)
    def _(j):
        tx, tz = neighbour(j)
        there = tx * 4 + lax.rem(tz, 4)
        remote(st.at[there], xst.at[core, j], SEM["xst0"] + core, at(tx, tz, hub))
        remote(nb.at[pl.ds(there * 4, 4)], xn.at[core, j], SEM["xn0"] + core, at(tx, tz, hub))

    @on_low
    def _():
        remote(st.at[block], xst.at[0, near], "xst0", at(x, z, hub))
        remote(nb.at[owned], xn.at[0, near], "xn0", at(x, z, hub))
        leaf_part(0)
        remote(leaf.at[0], leaf.at[0], "leaf", at(x, z, hub))

    aa, a0 = r["aa"], r["a0"]
    upper = lax.broadcasted_iota(jnp.int32, (8, 128), 0)
    lane8 = lax.broadcasted_iota(jnp.int32, (8, 128), 1)
    lane = lax.broadcasted_iota(jnp.int32, (1, 128), 1)
    maximum_lane = lane % 16 < 8
    my_maxima = (lane >= 16 * turn) & (lane < 16 * turn + 8)

    def upright(row, i):
        spread = jnp.broadcast_to(row, (8, 128))
        return jnp.sum(jnp.where(lane8 == upper + 16 * i, spread, 0.0), axis=1, keepdims=True)

    def flat(col, at_lane):
        spread = jnp.broadcast_to(col, (8, 128))
        return jnp.sum(jnp.where(lane8 == upper + at_lane, spread, 0.0), axis=0, keepdims=True)

    def onward(factors):
        return pltpu.roll(factors, 8, 1)

    def extra_of(p):
        query = qa[mine] if p else q0[turn]
        new = tkv[turn, p] + fkv[0, p] + fkv[1, p] + fkv[2, p]
        new = new.astype(BF16).astype(F32)
        own_m = jnp.sum(query.astype(F32) * new[:, :head_size], axis=1, keepdims=True) * scale
        leaf_m, leaf_l = leaf[p, 0][:, :1], leaf[p, 1][:, :1]
        top = jnp.maximum(own_m, leaf_m)
        own_f, leaf_f = jnp.exp(own_m - top), jnp.exp(leaf_m - top)
        total = own_f + leaf_f * leaf_l
        extra = flat(top, 16 * turn) + flat(total, 16 * turn + 8)
        extra = jnp.where(maximum_lane & ~my_maxima, NEGATIVE, extra)
        return extra, own_f * new[:, head_size:] + leaf_f * leaf[p, 2]

    @on_hub
    def _():
        xst[1, near] = st[block]
        xn[1, near] = nb[owned]
        arrive("fkv", fkv)
        extras = extra_of(1)
        for p in (1, 0):
            arrive("xst1" if p else "xst0", xst.at[1, fifteen] if p else xst.at[0])
            stats, (extra, extra_n) = xst[p, :, 0, :], extras
            top = jnp.maximum(jnp.max(stats, axis=0, keepdims=True), extra)
            factors = jnp.exp(stats - top)
            extra_f = jnp.where(my_maxima, jnp.exp(extra - top), 0.0)
            total = jnp.sum(onward(factors) * stats, axis=0, keepdims=True)
            total = total + onward(extra_f) * extra
            fs[turn, p] = jnp.where(maximum_lane, top, total)
            for tz in distant:
                remote(fs.at[turn, p], fs.at[turn, p], "fs1" if p else "fs0", at(x, tz, hd))
            arrive("xn1" if p else "xn0", xn.at[1, fifteen] if p else xn.at[0])
            for i in range(4):
                summed = upright(extra_f, i) * extra_n
                for s in range(near + 1):
                    summed = summed + upright(factors[s : s + 1], i) * xn[p, s, i].astype(F32)
                fn[turn, p, i] = summed.astype(BF16)
            for tz in distant:
                remote(fn.at[turn, p], fn.at[turn, p], "fn1" if p else "fn0", at(x, tz, hd))
            if p:
                arrive("leaf", leaf.at[0])
                extras = extra_of(0)

        for p in (1, 0):
            arrive("fs1" if p else "fs0", fs.at[three, p])
            stats = fs[:, p, 0, :]
            top = jnp.max(stats, axis=0, keepdims=True)
            f = jnp.exp(stats - top)
            total = pltpu.roll(jnp.sum(onward(f) * stats, axis=0, keepdims=True), 120, 1)
            f = f / jnp.where(maximum_lane & (lane < 64), total, 1.0)
            f = [[upright(f[s : s + 1], i) for s in range(4)] for i in range(4)]
            arrive("fn1" if p else "fn0", fn.at[three, p])
            for i in range(4):
                attended = sum(f[i][s] * fn[s, p, i].astype(F32) for s in range(4))
                if p:
                    aa[block * 4 + i] = attended.astype(BF16)
                else:
                    a0[i] = attended.astype(BF16)
            if p:

                @pl.loop(0, near)
                def _(j):
                    tx, tz = neighbour(j)
                    remote(aa.at[owned], aa.at[owned], "aa1", at(tx, tz, hd))

        @pl.loop(0, near)
        def _(j):
            tx, tz = neighbour(j)
            remote(a0, aa.at[owned], "aa0", at(tx, tz, low))

        remote(a0, aa.at[owned], "aa0", at(x, z, low))

    loads["wo"].wait()

    @on_hub
    def _():
        arrive("aa1", aa.at[pl.ds(0, near * 4)])

    @on_low
    def _():
        arrive("aa0", aa)

    for n in range(nodes):
        qf[n] = aa[rho(n)].astype(F32)
    acc = jnp.zeros((nodes, out_width), F32)
    for h in range(heads):
        acc = acc + dot_t(qf[:, h, :].astype(BF16), r["wo"][:, h * head_size : (h + 1) * head_size])
    rows_out = nodes // heads_n
    os, orr = r["os"], r["orr"]
    os[:, :, pl.ds(0, out_width)] = acc.reshape(heads_n, rows_out, out_width)
    for dh in (4, 3, 5, 2, 6, 1, 7):
        th = lax.rem(hd + dh, heads_n)
        remote(os.at[th], orr.at[dh - 1], "out", {"nodes": me, "heads": th})
    arrive("out", orr)
    result = os[hd] + jnp.sum(orr[...], axis=0)
    r["out"][...] = result[:, :out_width].astype(BF16)

    left("out", orr)

    @on_low
    def _():
        left("nq0", nq.at[0])
        left("xkv0", xkv.at[0])
        left("leaf", leaf.at[0])
        left("xst0", xst.at[0])
        left("xn0", xn.at[0])

    @on_hub
    def _():
        left("rows", cols.at[pl.ds(0, nodes - 1)])
        left("twin", cols)
        left("nq1", nq.at[1, fifteen])
        left("fq0", fq.at[three, 0])
        left("fq1", fq.at[three, 1])
        left("qa0", qa)
        left("qa1", qa.at[pl.ds(0, near * 4)])
        left("xkv1", xkv.at[1, three])
        left("nkv", nkv)
        left("fkv", fkv)
        left("xst1", xst.at[1, fifteen])
        left("xn1", xn.at[1, fifteen])
        left("fs0", fs.at[three, 0])
        left("fs1", fs.at[three, 1])
        left("fn0", fn.at[three, 0])
        left("fn1", fn.at[three, 1])
        left("aa0", aa)
        left("aa1", aa.at[pl.ds(0, near * 4)])


def on_device(
    hidden,
    norm_gain,
    qkv_weight,
    out_weight,
    prefix_keys,
    prefix_values,
    leaf_keys,
    leaf_values,
    piece_node,
    mid_parent,
    leaf_parent,
    leaf_len,
    sink_len,
    window_len,
):
    nodes = lax.axis_size("nodes")
    heads_n = lax.axis_size("heads")
    xs = nodes // ZS
    width, heads, triple = qkv_weight.shape
    head_size = triple // 3
    seg_dev, seg = prefix_keys.shape[:2]
    leaf_max = leaf_keys.shape[1]
    out_width = out_weight.shape[1]
    rows_out = nodes // heads_n
    dims = (nodes, heads_n, heads, head_size, width, seg_dev, seg, leaf_max, out_width)
    large = {
        "hidden_hbm": hidden,
        "gain_hbm": norm_gain[None, :],
        "pn_hbm": piece_node[None, :],
        "mp_hbm": mid_parent[None, :],
        "lp_hbm": leaf_parent[None, :],
        "ll_hbm": leaf_len[None, :],
        "sl_hbm": sink_len[None, :],
        "wl_hbm": window_len[None, :],
        "w_hbm": qkv_weight.transpose(1, 0, 2),
        "wo_hbm": out_weight.T,
        "k_hbm": prefix_keys.transpose(0, 2, 1, 3),
        "v_hbm": prefix_values.transpose(0, 2, 1, 3),
        "lk_hbm": leaf_keys[0].transpose(1, 0, 2),
        "lv_hbm": leaf_values[0].transpose(1, 0, 2),
    }
    vmem = pltpu.VMEM
    scratch = {n[:-4]: vmem(a.shape, a.dtype) for n, a in large.items()}
    scratch |= {
        "rows": vmem((nodes, 1, 128), F32),
        "cols": vmem((nodes, 1, 128), F32),
        "mask": vmem((nodes, seg_dev * seg), F32),
        "leaf_mask": vmem((8, leaf_max), F32),
        "pq": vmem((nodes, 8, head_size), F32),
        "nq": vmem((2, xs * 4, 4, 8, head_size), F32),
        "fq": vmem((4, 2, 4, 8, head_size), F32),
        "pkv": vmem((nodes, 8, 2 * head_size), F32),
        "pkv16": vmem((nodes, 8, 2 * head_size), BF16),
        "xkv": vmem((2, xs, ZS, 8, 2 * head_size), BF16),
        "skv": vmem((ZS, 2, 8, 2 * head_size), F32),
        "nkv": vmem((3, 4, 2, 8, 2 * head_size), F32),
        "tkv": vmem((4, 2, 8, 2 * head_size), F32),
        "fkv": vmem((3, 2, 8, 2 * head_size), F32),
        "q0": vmem((4, 8, head_size), BF16),
        "a0": vmem((4, 8, head_size), BF16),
        "leaf": vmem((2, 3, 8, head_size), F32),
        "qa": vmem((nodes, 8, head_size), BF16),
        "aa": vmem((nodes, 8, head_size), BF16),
        "qf": vmem((nodes, 8, head_size), F32),
        "nb32": vmem((nodes, 8, head_size), F32),
        "nb": vmem((nodes, 8, head_size), BF16),
        "xn": vmem((2, xs * 4, 4, 8, head_size), BF16),
        "st32": vmem((nodes, 128), F32),
        "st": vmem((nodes // 4, 1, 128), F32),
        "xst": vmem((2, xs * 4, 1, 128), F32),
        "fn": vmem((4, 2, 4, 8, head_size), BF16),
        "fs": vmem((4, 2, 1, 128), F32),
        "os": vmem((heads_n, rows_out, 128), F32),
        "orr": vmem((heads_n - 1, rows_out, 128), F32),
        "load": pltpu.SemaphoreType.DMA((len(LOADED),)),
        "send": pltpu.SemaphoreType.DMA((len(SEM),)),
        "recv": pltpu.SemaphoreType.DMA((len(SEM),)),
    }
    names = list(large) + ["out"] + list(scratch)
    return pl.pallas_call(
        functools.partial(kernel, dims, names),
        out_shape=jax.ShapeDtypeStruct((rows_out, out_width), BF16),
        in_specs=[pl.BlockSpec(memory_space=pl.ANY)] * len(large),
        out_specs=pl.BlockSpec(memory_space=pltpu.VMEM),
        scratch_shapes=list(scratch.values()),
        compiler_params=pltpu.CompilerParams(
            collective_id=0, has_side_effects=True, vmem_limit_bytes=60 * 2**20
        ),
    )(*large.values())


def solution(mesh):
    return jax.shard_map(
        on_device,
        mesh=mesh,
        in_specs=(
            P("nodes", None),
            P(),
            P("nodes", "heads", None),
            P("heads", "nodes"),
            P("nodes", None, "heads", None),
            P("nodes", None, "heads", None),
            P("nodes", None, "heads", None),
            P("nodes", None, "heads", None),
            P(),
            P(),
            P(),
            P(),
            P(),
            P(),
        ),
        out_specs=P("heads", "nodes"),
        check_vma=False,
    )
```

```python
import functools
import math

import jax
import jax.numpy as jnp
from jax import lax
from jax.experimental import pallas as pl
from jax.experimental.pallas import tpu as pltpu
from jax.sharding import PartitionSpec as P

MESH = pl.DeviceIdType.MESH
F32 = jnp.float32
BF16 = jnp.bfloat16
ROOTS = 4
EPSILON = 1e-05
NEGATIVE = -1e30
LOADED = ("hidden", "gain", "pn", "mp", "lp", "ll", "sl", "wl", "w", "k", "v", "lk", "lv", "wo")
SEM = {
    n: i
    for i, n in enumerate(
        ("rows", "twin", "nq0", "nq1", "fq0", "fq1", "qa0", "qa1", "xkv0", "xkv1", "nkv", "fkv", "leaf")
        + ("xst0", "xst1", "xn0", "xn1", "fs0", "fs1", "fn0", "fn1", "aa0", "aa1", "out")
    )
}
ZS = 16


def rho(n):
    z = lax.rem(n, ZS) if not isinstance(n, int) else n % ZS
    return n - z + (z % 4) * 4 + z // 4


def column(row):
    n = row.shape[1]
    i = lax.broadcasted_iota(jnp.int32, (n, n), 0)
    here = (i // ZS) * ZS + (i % 4) * 4 + (i % ZS) // 4 == lax.broadcasted_iota(jnp.int32, (n, n), 1)
    return jnp.sum(jnp.where(here, jnp.broadcast_to(row, (n, n)), 0.0), axis=1, keepdims=True)


def dot_t(a, b):
    return lax.dot_general(a, b, (((1,), (1,)), ((), ())), preferred_element_type=F32)


def dot(a, b):
    return jnp.dot(a, b, preferred_element_type=F32)


def kernel(dims, names, *refs):
    nodes, heads_n, heads, head_size, width, seg_dev, seg, leaf_max, out_width = dims
    r = dict(zip(names, refs, strict=True))
    xs = nodes // ZS
    me = lax.axis_index("nodes")
    hd = lax.axis_index("heads")
    x, z = me // ZS, lax.rem(me, ZS)
    core = lax.rem(hd, 2)
    hub, low, twin = hd + 1 - core, hd - core, hd + 1 - 2 * core
    mine, block, turn = rho(me), x * 4 + lax.rem(z, 4), z // 4
    scale = 1.0 / math.sqrt(head_size)
    near = xs * 4 - 1
    owned = pl.ds(block * 4, 4)
    fifteen, three = pl.ds(0, near), pl.ds(0, 3)

    def at(tx, tz, th):
        return {"nodes": tx * ZS + tz, "heads": th}

    def far(j):
        half = (j + 1) // 2
        return lax.rem(z + ZS // 2 + half * (1 - 2 * lax.rem(j, 2)), ZS)

    def across(j):
        return lax.rem(x + j, xs)

    def offsets_of(j):
        i, k = lax.rem(j, 4), j // 4
        return 2 + ((i + 1) // 2) * (1 - 2 * lax.rem(i, 2)), 2 - k - k // 2 + 2 * (k // 3)

    def neighbour(j):
        dx, dz = offsets_of(j)
        return lax.rem(x + dx, xs), lax.rem(z + dz + ZS, ZS)

    def copy(src, dst, sem, target):
        return pltpu.make_async_remote_copy(
            src_ref=src,
            dst_ref=dst,
            send_sem=r["send"].at[sem],
            recv_sem=r["recv"].at[sem],
            device_id=target,
            device_id_type=MESH,
        )

    def remote(src, dst, sem, target):
        copy(src, dst, SEM[sem] if isinstance(sem, str) else sem, target).start()

    def arrive(sem, ref):
        copy(ref, ref, SEM[sem], at(x, z, twin)).wait_recv()

    def left(sem, ref):
        copy(ref, ref, SEM[sem], at(x, z, twin)).wait_send()

    on_hub, on_low = pl.when(core == 1), pl.when(core == 0)
    distant = [lax.rem(z + 4 * d, ZS) for d in (2, 1, 3)]

    loads = {
        n: pltpu.make_async_copy(r[n + "_hbm"], r[n], r["load"].at[i])
        for i, n in enumerate(LOADED)
    }
    loads["hidden"].start()
    loads["gain"].start()
    barrier = pltpu.get_barrier_semaphore()

    def tell(target):
        pl.semaphore_signal(barrier, inc=1, device_id=target, device_id_type=MESH)

    @on_hub
    def _():
        @pl.loop(0, ZS - 1)
        def _(j):
            for dx in (2, 1, 3, 0):
                tell(at(across(dx), far(j), hd))

        for dx in range(1, xs):
            tell(at(across(dx), z, hd))

    @pl.loop(0, near)
    def _(j):
        dx, dz = offsets_of(j)
        tell(at(lax.rem(x - dx + 2 * xs, xs), lax.rem(z - dz + ZS, ZS), twin))

    for dh in range(1, heads_n):
        tell({"nodes": me, "heads": lax.rem(hd + dh, heads_n)})

    for n in LOADED[2:]:
        loads[n].start()
    loads["hidden"].wait()
    loads["gain"].wait()

    rows, cols = r["rows"], r["cols"]

    @on_hub
    def _():
        values = r["hidden"][...].astype(F32)
        features = values.shape[1]
        mean = jnp.sum(values, axis=1, keepdims=True) * (1.0 / features)
        centered = values - mean
        variance = jnp.sum(centered * centered, axis=1, keepdims=True) * (1.0 / features)
        normed = centered * lax.rsqrt(variance + EPSILON) * r["gain"][...]
        normed = normed.astype(BF16).astype(F32)
        for n in range(nodes):
            rows[n, :, pl.ds(0, width)] = normed[:, n * width : (n + 1) * width]

        pl.semaphore_wait(barrier, nodes - 1 + near + heads_n - 1)

        @pl.loop(0, ZS - 1)
        def _(j):
            tz = far(j)
            for dx in (2, 1, 3, 0):
                tx = across(dx)
                remote(rows.at[tx * ZS + tz], cols.at[mine], "rows", at(tx, tz, hd))

        for dx in range(1, xs):
            tx = across(dx)
            remote(rows.at[tx * ZS + z], cols.at[mine], "rows", at(tx, z, hd))
        cols[mine] = rows[me]

    @on_low
    def _():
        pl.semaphore_wait(barrier, near + heads_n - 1)

    for n in ("pn", "mp", "lp", "ll", "sl", "wl"):
        loads[n].wait()
    pn = r["pn"][...].astype(F32)
    pieces = pn.shape[1]
    mids = r["mp"].shape[1]
    parent = column(r["lp"][...].astype(F32))
    leaf_len = column(r["ll"][...].astype(F32))
    sink = column(r["sl"][...].astype(F32))
    window = column(r["wl"][...].astype(F32))
    mid_ids = lax.broadcasted_iota(jnp.int32, (nodes, mids), 1).astype(F32)
    mp = jnp.broadcast_to(r["mp"][...].astype(F32), (nodes, mids))
    root_node = jnp.sum(jnp.where(mid_ids == parent, mp, 0.0), axis=1, keepdims=True)
    mid_node = parent + float(ROOTS)
    pn_all = jnp.broadcast_to(pn, (nodes, pieces))
    root_len = float(seg) * jnp.sum(jnp.where(pn_all == root_node, 1.0, 0.0), axis=1, keepdims=True)
    mid_len = float(seg) * jnp.sum(jnp.where(pn_all == mid_node, 1.0, 0.0), axis=1, keepdims=True)
    finish = root_len + mid_len + leaf_len
    since = finish - window
    piece_ids = lax.broadcasted_iota(jnp.int32, (1, pieces), 1)
    offsets = lax.broadcasted_iota(jnp.int32, (nodes, seg), 1).astype(F32)
    for p in range(seg_dev):
        here = me * seg_dev + p
        node = jnp.sum(jnp.where(piece_ids == here, pn, 0.0), axis=1, keepdims=True)
        same = (pn == node) & (piece_ids < here)
        rank = jnp.sum(jnp.where(same, 1.0, 0.0), axis=1, keepdims=True)
        at_mid = mid_node == node
        start = jnp.where(at_mid, root_len, 0.0) + rank * float(seg)
        position = offsets + start
        visible = ((position < sink) | (position >= since)) & (at_mid | (root_node == node))
        r["mask"][:, p * seg : (p + 1) * seg] = jnp.where(visible, 1.0, 0.0)
    my_row = lax.broadcasted_iota(jnp.int32, (nodes, 1), 0) == mine

    def mine_of(values):
        return jnp.sum(jnp.where(my_row, values, 0.0), axis=0, keepdims=True)

    my_finish, my_leaf, my_sink = mine_of(finish), mine_of(leaf_len), mine_of(sink)
    my_low = mine_of(since)
    leaf_offsets = lax.broadcasted_iota(jnp.int32, (8, leaf_max), 1).astype(F32)
    leaf_position = leaf_offsets + (my_finish - my_leaf)
    leaf_visible = ((leaf_position < my_sink) | (leaf_position >= my_low)) & (leaf_offsets < my_leaf)
    r["leaf_mask"][...] = jnp.where(leaf_visible, 1.0, 0.0)

    pq, pkv = r["pq"], r["pkv"]
    pq[:, heads, :] = jnp.zeros((nodes, head_size), F32)
    pkv[:, heads, :] = jnp.zeros((nodes, 2 * head_size), F32)
    loads["w"].wait()

    @on_hub
    def _():
        arrive("rows", cols.at[pl.ds(0, nodes - 1)])
        remote(cols, cols, "twin", at(x, z, low))

    @on_low
    def _():
        arrive("twin", cols)

    lhs = cols[:, 0, :][:, :width].astype(BF16)
    for h in range(heads):
        pq[:, h, :] = dot(lhs, r["w"][h, :, pl.ds(0, head_size)])
    nq, fq = r["nq"], r["fq"]

    @pl.loop(0, near)
    def _(j):
        tx, tz = neighbour(j)
        src = pq.at[pl.ds((tx * 4 + lax.rem(tz, 4)) * 4, 4)]
        remote(src, nq.at[core, j], SEM["nq0"] + core, at(tx, tz, hub))

    @on_low
    def _():
        remote(pq.at[owned], nq.at[0, near], "nq0", at(x, z, hub))

    for h in range(heads):
        pkv[:, h, :] = dot(lhs, r["w"][h, :, pl.ds(head_size, 2 * head_size)])
    pkv16 = r["pkv16"]
    pkv16[...] = pkv[...].astype(BF16)

    xkv, skv, nkv, tkv, fkv = r["xkv"], r["skv"], r["nkv"], r["tkv"], r["fkv"]
    row = pl.ds(x * ZS, ZS)
    @on_low
    def _():
        for dx in range(1, xs):
            tx = across(dx)
            remote(pkv16.at[pl.ds(tx * ZS, ZS)], xkv.at[0, dx - 1], "xkv0", at(tx, z, hub))
        remote(pkv16.at[row], xkv.at[0, xs - 1], "xkv0", at(x, z, hub))

    @on_hub
    def _():
        nq[1, near] = pq[owned]
        arrive("nq1", nq.at[1, fifteen])
        fq[turn, 1] = jnp.sum(nq[1], axis=0)
        for tz in distant:
            remote(fq.at[turn, 1], fq.at[turn, 1], "fq1", at(x, tz, hd))
        for dx in range(1, xs):
            tx = across(dx)
            remote(pkv16.at[pl.ds(tx * ZS, ZS)], xkv.at[1, dx - 1], "xkv1", at(tx, z, hd))
        arrive("nq0", nq.at[0])
        fq[turn, 0] = jnp.sum(nq[0], axis=0)
        for tz in distant:
            remote(fq.at[turn, 0], fq.at[turn, 0], "fq0", at(x, tz, hd))

    qa, q0 = r["qa"], r["q0"]
    row_ids = lax.broadcasted_iota(jnp.int32, (8, 1), 0)
    leaf = r["leaf"]

    def leaf_part(at_core):
        query = qa[mine]
        scores = jnp.zeros((8, leaf_max), F32)
        for h in range(heads):
            scores = jnp.where(row_ids == h, dot_t(query, r["lk"][h]), scores)
        on = r["leaf_mask"][...] > 0.0
        scores = jnp.where(on, scores * scale, NEGATIVE)
        top = jnp.max(scores, axis=1, keepdims=True)
        weights = jnp.where(on, jnp.exp(scores - top), 0.0).astype(BF16)
        summed = jnp.zeros((8, head_size), F32)
        for h in range(heads):
            summed = jnp.where(row_ids == h, dot(weights, r["lv"][h]), summed)
        total = jnp.sum(weights.astype(F32), axis=1, keepdims=True)
        leaf[at_core, 0] = jnp.broadcast_to(top, (8, head_size))
        leaf[at_core, 1] = jnp.broadcast_to(total, (8, head_size))
        leaf[at_core, 2] = summed

    for n in ("lk", "lv", "k", "v"):
        loads[n].wait()

    @on_hub
    def _():
        xkv[1, xs - 1] = pkv16[row]
        arrive("xkv1", xkv.at[1, three])
        arrive("xkv0", xkv.at[0])
        for p in range(2):
            skv[:, p] = jnp.sum(xkv[p].astype(F32), axis=0)
        for i, dz in enumerate((2, 1, -1)):
            tz = lax.rem(z + dz + ZS, ZS)
            remote(skv.at[pl.ds(lax.rem(tz, 4) * 4, 4)], nkv.at[i], "nkv", at(x, tz, hd))
        arrive("fq1", fq.at[three, 1])

        qa[owned] = (fq[0, 1] + fq[1, 1] + fq[2, 1] + fq[3, 1]).astype(BF16)

        @pl.loop(0, near)
        def _(j):
            tx, tz = neighbour(j)
            remote(qa.at[owned], qa.at[owned], "qa1", at(tx, tz, hd))

        arrive("fq0", fq.at[three, 0])
        q0[...] = (fq[0, 0] + fq[1, 0] + fq[2, 0] + fq[3, 0]).astype(BF16)

        @pl.loop(0, near)
        def _(j):
            tx, tz = neighbour(j)
            remote(q0, qa.at[owned], "qa0", at(tx, tz, low))

        remote(q0, qa.at[owned], "qa0", at(x, z, low))
        leaf_part(1)
        arrive("nkv", nkv)
        tkv[...] = skv[pl.ds(lax.rem(z, 4) * 4, 4)] + jnp.sum(nkv[...], axis=0)
        for i, tz in enumerate(distant):
            remote(tkv.at[tz // 4], fkv.at[i], "fkv", at(x, tz, hd))
        arrive("qa1", qa.at[pl.ds(0, near * 4)])

    @on_low
    def _():
        arrive("qa0", qa)

    qf = r["qf"]
    qf[...] = qa[...].astype(F32)
    lanes = lax.broadcasted_iota(jnp.int32, (nodes, 128), 1)
    base = 16 * (lax.broadcasted_iota(jnp.int32, (nodes, 128), 0) % 4)
    stats = jnp.zeros((nodes, 128), F32)
    nb32, nb, st = r["nb32"], r["nb"], r["st"]
    for h in range(heads):
        qh = qf[:, h, :].astype(BF16)
        on = r["mask"][...] > 0.0
        scores = jnp.concatenate([dot_t(qh, r["k"][p, h]) for p in range(seg_dev)], axis=1)
        scores = jnp.where(on, scores * scale, NEGATIVE)
        top = jnp.max(scores, axis=1, keepdims=True)
        weights = jnp.where(on, jnp.exp(scores - top), 0.0).astype(BF16)
        total = jnp.sum(weights.astype(F32), axis=1, keepdims=True)
        summed = dot(weights[:, :seg], r["v"][0, h])
        for p in range(1, seg_dev):
            summed = summed + dot(weights[:, p * seg : (p + 1) * seg], r["v"][p, h])
        nb32[:, h, :] = summed
        stats = jnp.where(lanes == base + h, top, stats)
        stats = jnp.where(lanes == base + (8 + h), total, stats)
    nb32[:, heads, :] = jnp.zeros((nodes, head_size), F32)
    nb[...] = nb32[...].astype(BF16)
    r["st32"][...] = stats
    st[:, 0, :] = sum(r["st32"][pl.ds(i, nodes // 4, stride=4), :] for i in range(4))

    xn, xst, fn, fs = r["xn"], r["xst"], r["fn"], r["fs"]

    @pl.loop(0, near)
    def _(j):
        tx, tz = neighbour(j)
        there = tx * 4 + lax.rem(tz, 4)
        remote(st.at[there], xst.at[core, j], SEM["xst0"] + core, at(tx, tz, hub))
        remote(nb.at[pl.ds(there * 4, 4)], xn.at[core, j], SEM["xn0"] + core, at(tx, tz, hub))

    @on_low
    def _():
        remote(st.at[block], xst.at[0, near], "xst0", at(x, z, hub))
        remote(nb.at[owned], xn.at[0, near], "xn0", at(x, z, hub))
        leaf_part(0)
        remote(leaf.at[0], leaf.at[0], "leaf", at(x, z, hub))

    aa, a0 = r["aa"], r["a0"]
    upper = lax.broadcasted_iota(jnp.int32, (8, 128), 0)
    lane8 = lax.broadcasted_iota(jnp.int32, (8, 128), 1)
    lane = lax.broadcasted_iota(jnp.int32, (1, 128), 1)
    maximum_lane = lane % 16 < 8
    my_maxima = (lane >= 16 * turn) & (lane < 16 * turn + 8)

    def upright(row, i):
        spread = jnp.broadcast_to(row, (8, 128))
        return jnp.sum(jnp.where(lane8 == upper + 16 * i, spread, 0.0), axis=1, keepdims=True)

    def flat(col, at_lane):
        spread = jnp.broadcast_to(col, (8, 128))
        return jnp.sum(jnp.where(lane8 == upper + at_lane, spread, 0.0), axis=0, keepdims=True)

    def onward(factors):
        return pltpu.roll(factors, 8, 1)

    def extra_of(p):
        query = qa[mine] if p else q0[turn]
        new = tkv[turn, p] + fkv[0, p] + fkv[1, p] + fkv[2, p]
        new = new.astype(BF16).astype(F32)
        own_m = jnp.sum(query.astype(F32) * new[:, :head_size], axis=1, keepdims=True) * scale
        leaf_m, leaf_l = leaf[p, 0][:, :1], leaf[p, 1][:, :1]
        top = jnp.maximum(own_m, leaf_m)
        own_f, leaf_f = jnp.exp(own_m - top), jnp.exp(leaf_m - top)
        total = own_f + leaf_f * leaf_l
        extra = flat(top, 16 * turn) + flat(total, 16 * turn + 8)
        extra = jnp.where(maximum_lane & ~my_maxima, NEGATIVE, extra)
        return extra, own_f * new[:, head_size:] + leaf_f * leaf[p, 2]

    @on_hub
    def _():
        xst[1, near] = st[block]
        xn[1, near] = nb[owned]
        arrive("fkv", fkv)
        extras = extra_of(1)
        for p in (1, 0):
            arrive("xst1" if p else "xst0", xst.at[1, fifteen] if p else xst.at[0])
            stats, (extra, extra_n) = xst[p, :, 0, :], extras
            top = jnp.maximum(jnp.max(stats, axis=0, keepdims=True), extra)
            factors = jnp.exp(stats - top)
            extra_f = jnp.where(my_maxima, jnp.exp(extra - top), 0.0)
            total = jnp.sum(onward(factors) * stats, axis=0, keepdims=True)
            total = total + onward(extra_f) * extra
            fs[turn, p] = jnp.where(maximum_lane, top, total)
            for tz in distant:
                remote(fs.at[turn, p], fs.at[turn, p], "fs1" if p else "fs0", at(x, tz, hd))
            arrive("xn1" if p else "xn0", xn.at[1, fifteen] if p else xn.at[0])
            for i in range(4):
                summed = upright(extra_f, i) * extra_n
                for s in range(near + 1):
                    summed = summed + upright(factors[s : s + 1], i) * xn[p, s, i].astype(F32)
                fn[turn, p, i] = summed.astype(BF16)
            for tz in distant:
                remote(fn.at[turn, p], fn.at[turn, p], "fn1" if p else "fn0", at(x, tz, hd))
            if p:
                arrive("leaf", leaf.at[0])
                extras = extra_of(0)

        for p in (1, 0):
            arrive("fs1" if p else "fs0", fs.at[three, p])
            stats = fs[:, p, 0, :]
            top = jnp.max(stats, axis=0, keepdims=True)
            f = jnp.exp(stats - top)
            total = pltpu.roll(jnp.sum(onward(f) * stats, axis=0, keepdims=True), 120, 1)
            f = f / jnp.where(maximum_lane & (lane < 64), total, 1.0)
            f = [[upright(f[s : s + 1], i) for s in range(4)] for i in range(4)]
            arrive("fn1" if p else "fn0", fn.at[three, p])
            for i in range(4):
                attended = sum(f[i][s] * fn[s, p, i].astype(F32) for s in range(4))
                if p:
                    aa[block * 4 + i] = attended.astype(BF16)
                else:
                    a0[i] = attended.astype(BF16)
            if p:

                @pl.loop(0, near)
                def _(j):
                    tx, tz = neighbour(j)
                    remote(aa.at[owned], aa.at[owned], "aa1", at(tx, tz, hd))

        @pl.loop(0, near)
        def _(j):
            tx, tz = neighbour(j)
            remote(a0, aa.at[owned], "aa0", at(tx, tz, low))

        remote(a0, aa.at[owned], "aa0", at(x, z, low))

    loads["wo"].wait()

    @on_hub
    def _():
        arrive("aa1", aa.at[pl.ds(0, near * 4)])

    @on_low
    def _():
        arrive("aa0", aa)

    for n in range(nodes):
        qf[n] = aa[rho(n)].astype(F32)
    acc = jnp.zeros((nodes, out_width), F32)
    for h in range(heads):
        acc = acc + dot_t(qf[:, h, :].astype(BF16), r["wo"][:, h * head_size : (h + 1) * head_size])
    rows_out = nodes // heads_n
    os, orr = r["os"], r["orr"]
    os[:, :, pl.ds(0, out_width)] = acc.reshape(heads_n, rows_out, out_width)
    for dh in (4, 3, 5, 2, 6, 1, 7):
        th = lax.rem(hd + dh, heads_n)
        remote(os.at[th], orr.at[dh - 1], "out", {"nodes": me, "heads": th})
    arrive("out", orr)
    result = os[hd] + jnp.sum(orr[...], axis=0)
    r["out"][...] = result[:, :out_width].astype(BF16)

    left("out", orr)

    @on_low
    def _():
        left("nq0", nq.at[0])
        left("xkv0", xkv.at[0])
        left("leaf", leaf.at[0])
        left("xst0", xst.at[0])
        left("xn0", xn.at[0])

    @on_hub
    def _():
        left("rows", cols.at[pl.ds(0, nodes - 1)])
        left("twin", cols)
        left("nq1", nq.at[1, fifteen])
        left("fq0", fq.at[three, 0])
        left("fq1", fq.at[three, 1])
        left("qa0", qa)
        left("qa1", qa.at[pl.ds(0, near * 4)])
        left("xkv1", xkv.at[1, three])
        left("nkv", nkv)
        left("fkv", fkv)
        left("xst1", xst.at[1, fifteen])
        left("xn1", xn.at[1, fifteen])
        left("fs0", fs.at[three, 0])
        left("fs1", fs.at[three, 1])
        left("fn0", fn.at[three, 0])
        left("fn1", fn.at[three, 1])
        left("aa0", aa)
        left("aa1", aa.at[pl.ds(0, near * 4)])


def on_device(
    hidden,
    norm_gain,
    qkv_weight,
    out_weight,
    prefix_keys,
    prefix_values,
    leaf_keys,
    leaf_values,
    piece_node,
    mid_parent,
    leaf_parent,
    leaf_len,
    sink_len,
    window_len,
):
    nodes = lax.axis_size("nodes")
    heads_n = lax.axis_size("heads")
    xs = nodes // ZS
    width, heads, triple = qkv_weight.shape
    head_size = triple // 3
    seg_dev, seg = prefix_keys.shape[:2]
    leaf_max = leaf_keys.shape[1]
    out_width = out_weight.shape[1]
    rows_out = nodes // heads_n
    dims = (nodes, heads_n, heads, head_size, width, seg_dev, seg, leaf_max, out_width)
    large = {
        "hidden_hbm": hidden,
        "gain_hbm": norm_gain[None, :],
        "pn_hbm": piece_node[None, :],
        "mp_hbm": mid_parent[None, :],
        "lp_hbm": leaf_parent[None, :],
        "ll_hbm": leaf_len[None, :],
        "sl_hbm": sink_len[None, :],
        "wl_hbm": window_len[None, :],
        "w_hbm": qkv_weight.transpose(1, 0, 2),
        "wo_hbm": out_weight.T,
        "k_hbm": prefix_keys.transpose(0, 2, 1, 3),
        "v_hbm": prefix_values.transpose(0, 2, 1, 3),
        "lk_hbm": leaf_keys[0].transpose(1, 0, 2),
        "lv_hbm": leaf_values[0].transpose(1, 0, 2),
    }
    vmem = pltpu.VMEM
    scratch = {n[:-4]: vmem(a.shape, a.dtype) for n, a in large.items()}
    scratch |= {
        "rows": vmem((nodes, 1, 128), F32),
        "cols": vmem((nodes, 1, 128), F32),
        "mask": vmem((nodes, seg_dev * seg), F32),
        "leaf_mask": vmem((8, leaf_max), F32),
        "pq": vmem((nodes, 8, head_size), F32),
        "nq": vmem((2, xs * 4, 4, 8, head_size), F32),
        "fq": vmem((4, 2, 4, 8, head_size), F32),
        "pkv": vmem((nodes, 8, 2 * head_size), F32),
        "pkv16": vmem((nodes, 8, 2 * head_size), BF16),
        "xkv": vmem((2, xs, ZS, 8, 2 * head_size), BF16),
        "skv": vmem((ZS, 2, 8, 2 * head_size), F32),
        "nkv": vmem((3, 4, 2, 8, 2 * head_size), F32),
        "tkv": vmem((4, 2, 8, 2 * head_size), F32),
        "fkv": vmem((3, 2, 8, 2 * head_size), F32),
        "q0": vmem((4, 8, head_size), BF16),
        "a0": vmem((4, 8, head_size), BF16),
        "leaf": vmem((2, 3, 8, head_size), F32),
        "qa": vmem((nodes, 8, head_size), BF16),
        "aa": vmem((nodes, 8, head_size), BF16),
        "qf": vmem((nodes, 8, head_size), F32),
        "nb32": vmem((nodes, 8, head_size), F32),
        "nb": vmem((nodes, 8, head_size), BF16),
        "xn": vmem((2, xs * 4, 4, 8, head_size), BF16),
        "st32": vmem((nodes, 128), F32),
        "st": vmem((nodes // 4, 1, 128), F32),
        "xst": vmem((2, xs * 4, 1, 128), F32),
        "fn": vmem((4, 2, 4, 8, head_size), BF16),
        "fs": vmem((4, 2, 1, 128), F32),
        "os": vmem((heads_n, rows_out, 128), F32),
        "orr": vmem((heads_n - 1, rows_out, 128), F32),
        "load": pltpu.SemaphoreType.DMA((len(LOADED),)),
        "send": pltpu.SemaphoreType.DMA((len(SEM),)),
        "recv": pltpu.SemaphoreType.DMA((len(SEM),)),
    }
    names = list(large) + ["out"] + list(scratch)
    return pl.pallas_call(
        functools.partial(kernel, dims, names),
        out_shape=jax.ShapeDtypeStruct((rows_out, out_width), BF16),
        in_specs=[pl.BlockSpec(memory_space=pl.ANY)] * len(large),
        out_specs=pl.BlockSpec(memory_space=pltpu.VMEM),
        scratch_shapes=list(scratch.values()),
        compiler_params=pltpu.CompilerParams(
            collective_id=0, has_side_effects=True, vmem_limit_bytes=60 * 2**20
        ),
    )(*large.values())


def solution(mesh):
    return jax.shard_map(
        on_device,
        mesh=mesh,
        in_specs=(
            P("nodes", None),
            P(),
            P("nodes", "heads", None),
            P("heads", "nodes"),
            P("nodes", None, "heads", None),
            P("nodes", None, "heads", None),
            P("nodes", None, "heads", None),
            P("nodes", None, "heads", None),
            P(),
            P(),
            P(),
            P(),
            P(),
            P(),
        ),
        out_specs=P("heads", "nodes"),
        check_vma=False,
    )
```
